768 devices in a mesh: tile: 96 (over y_lo, x, z), chan: 8 (over y_hi, core).
Axes of the slice: x: 4, y: 8 (y_hi: 4, y_lo: 2; y = y_hi * 2 + y_lo), z: 12, core: 2. Of those that a mesh axis runs over, the one named last changes fastest.
Arguments:
- inputs: bfloat16 [96, 256, 1024], P('tile', 'chan'), may hold values from -6 to 6
- grad_out: bfloat16 [96, 256, 1024], P('tile', 'chan'), may hold values from -6 to 6
- kernel: bfloat16 [25, 256], P(None, 'chan'), may hold values from -1.25 to 1.25
- w_in: bfloat16 [256, 1024], replicated, may hold values from -0.375 to 0.375
- w_out: bfloat16 [1024, 256], replicated, may hold values from -0.1875 to 0.1875
- neighbours: int32 [96, 8], replicated, may hold values from 0 to 95, as said below
- rotations: int32 [96, 8], replicated, may hold values from 0 to 3, as said below
Outputs:
- outputs: bfloat16 [96, 256, 1024], P('tile', 'chan')
- grad_in: bfloat16 [96, 256, 1024], P('tile', 'chan')
- grad_w_in: float32 [256, 1024], replicated
- grad_w_out: float32 [1024, 256], replicated
- grad_kernel: float32 [25, 256], replicated
The draws below stay inside these ranges and needn't reach their ends.
Inputs may be any that keep to these rules, and one draw needn't show every extreme that they name: neighbours[t, d] is the tile that borders tile t in direction d; for every tile t and direction d exactly one tile s has neighbours[s, d] = t, namely s = neighbours[t, 7 - d]. rotations[t, d] is the number of quarter turns that brings the bordering tile into tile t's frame.
All inputs are finite; a program needn't handle non-finite values.
Results may differ from the reference program's by a relative error of at most 0.006.
Values may be sent and summed in bfloat16 or wider, within the bound.
A program may use at most 64 MiB of HBM per device.

```python
import jax
import jax.numpy as jnp
from jax import lax

C = 256
HID = 1024
KSIZE = 5
SIDE = 32
PIX = 1024
TILES = 96


offsets = ((-1, -1), (-1, 0), (-1, 1), (0, -1), (0, 1), (1, -1), (1, 0), (1, 1))


def tile_layout(key):
    grid_cols = 4
    grid_rows = TILES // grid_cols
    placement = jax.random.permutation(jax.random.fold_in(key, 11), TILES).astype(jnp.int32)
    tile_at = jnp.zeros((TILES,), jnp.int32).at[placement].set(jnp.arange(TILES, dtype=jnp.int32))
    cell_row = placement // grid_cols
    cell_col = placement % grid_cols
    columns = []
    for step_row, step_col in offsets:
        grid_cell = (cell_row + step_row) % grid_rows * grid_cols + (cell_col + step_col) % grid_cols
        columns.append(tile_at[grid_cell])
    neighbour_table = jnp.stack(columns, axis=1).astype(jnp.int32)
    shuffled = jax.random.permutation(jax.random.fold_in(key, 23), TILES * 8).astype(jnp.int32)
    turn_codes = (shuffled % 4).reshape(TILES, 8).astype(jnp.int32)
    return (neighbour_table, turn_codes)


def draw_neighbours(key, part):
    return tile_layout(key)[0]


def draw_rotations(key, part):
    return tile_layout(key)[1]


def shard_levels(own_key, extent, split, least, largest):
    loudness, own = 1.0, jax.random.fold_in(own_key, 6)
    for position, shards_of in split:
        heights = jnp.exp(jax.random.uniform(jax.random.fold_in(own, position), (shards_of,), jnp.float32, least / len(split), largest / len(split)))
        loudness = loudness * jnp.repeat(heights, extent[position] // shards_of).reshape([-1 if axis == position else 1 for axis in range(len(extent))])
    return loudness


def noise(rng, extent, deviation, most, split=(), kind=jnp.bfloat16):
    values = jax.random.normal(rng, extent, jnp.float32) * deviation
    if len(split) > 0:
        values = shard_levels(rng, extent, split, -0.22, 0.18) * values
    return jnp.clip(values, min=-most, max=most).astype(kind)


def setup_inputs(seed: int = 0) -> dict:
    key_list = jax.random.split(jax.random.key(seed), 8)
    return {
        "inputs": noise(key_list[0], (TILES, C, PIX), 1.0, 6.0, ((0, 96), (1, 8))),
        "grad_out": noise(key_list[1], (TILES, C, PIX), 1.0, 6.0, ((0, 96), (1, 8))),
        "kernel": noise(key_list[2], (KSIZE * KSIZE, C), (KSIZE * KSIZE) ** -0.5, 1.25, ((1, 8),)),
        "w_in": noise(key_list[3], (C, HID), C ** -0.5, 0.375),
        "w_out": noise(key_list[4], (HID, C), HID ** -0.5, 0.1875),
        "neighbours": draw_neighbours(jax.random.fold_in(key_list[7], 71), 0),
        "rotations": draw_rotations(jax.random.fold_in(key_list[7], 71), 0),
    }


offsets = ((-1, -1), (-1, 0), (-1, 1), (0, -1), (0, 1), (1, -1), (1, 0), (1, 1))


def source_span(step_dir, edge_len, halo_width):
    if step_dir < 0:
        return (edge_len - halo_width, edge_len)
    if step_dir > 0:
        return (0, halo_width)
    return (0, edge_len)


def target_span(step_dir, edge_len, halo_width):
    if step_dir < 0:
        return (0, halo_width)
    if step_dir > 0:
        return (halo_width + edge_len, edge_len + 2 * halo_width)
    return (halo_width, halo_width + edge_len)


def rotate_tile(images, quarter):
    turn_code = jnp.reshape(quarter, quarter.shape + (1,) * (images.ndim - quarter.ndim))
    result = images
    for amount in range(1, 4):
        result = jnp.where(turn_code == amount, jnp.rot90(images, amount, axes=(-2, -1)), result)
    return result


def depthwise(padded, kernel, edge_len):
    result = jnp.zeros(padded.shape[:-2] + (edge_len, edge_len), jnp.float32)
    for tap_row in range(KSIZE):
        for tap_col in range(KSIZE):
            weight = kernel[tap_row * KSIZE + tap_col].astype(jnp.float32)[:, None, None]
            result = result + weight * padded[..., tap_row:tap_row + edge_len, tap_col:tap_col + edge_len].astype(jnp.float32)
    return result


def spread(grads, kernel, row_span, col_span):
    margin = KSIZE - 1
    widths = [(0, 0)] * (grads.ndim - 2) + [(margin, margin), (margin, margin)]
    widened = jnp.pad(grads, widths)
    result = jnp.zeros(grads.shape[:-2] + (row_span[1] - row_span[0], col_span[1] - col_span[0]), jnp.float32)
    for tap_row in range(KSIZE):
        for tap_col in range(KSIZE):
            weight = kernel[tap_row * KSIZE + tap_col].astype(jnp.float32)[:, None, None]
            result = result + weight * widened[..., row_span[0] + margin - tap_row:row_span[1] + margin - tap_row,
                                               col_span[0] + margin - tap_col:col_span[1] + margin - tap_col]
    return result


def kernel_grads(grad_tiles, padded, edge_len, sum_axes):
    columns = []
    for tap_row in range(KSIZE):
        for tap_col in range(KSIZE):
            window = padded[..., tap_row:tap_row + edge_len, tap_col:tap_col + edge_len].astype(jnp.float32)
            columns.append(jnp.sum(grad_tiles * window, axis=sum_axes))
    return jnp.stack(columns, axis=0)


def gelu_slope(values):
    cumul = 0.5 * (1.0 + lax.erf(values * 0.7071067811865476))
    return cumul + values * jnp.exp(-0.5 * values * values) * 0.3989422804014327


def reference(inputs, grad_out, kernel, w_in, w_out, neighbours, rotations):
    halo_width = KSIZE // 2
    ext_len = SIDE + 2 * halo_width
    images = inputs.reshape(TILES, C, SIDE, SIDE)
    padded = jnp.zeros((TILES, C, ext_len, ext_len), jnp.bfloat16)
    padded = padded.at[:, :, halo_width:halo_width + SIDE, halo_width:halo_width + SIDE].set(images)
    for direction, (step_row, step_col) in enumerate(offsets):
        turned = rotate_tile(images[neighbours[:, direction]], rotations[:, direction])
        src_rows = source_span(step_row, SIDE, halo_width)
        src_cols = source_span(step_col, SIDE, halo_width)
        dst_rows = target_span(step_row, SIDE, halo_width)
        dst_cols = target_span(step_col, SIDE, halo_width)
        padded = padded.at[:, :, dst_rows[0]:dst_rows[1], dst_cols[0]:dst_cols[1]].set(
            turned[:, :, src_rows[0]:src_rows[1], src_cols[0]:src_cols[1]])
    hidden = depthwise(padded, kernel, SIDE).astype(jnp.bfloat16).reshape(TILES, C, PIX)

    def per_tile(running, tile_pair):
        features, cotangent = tile_pair
        pre_act = lax.dot_general(w_in, features, (((0,), (0,)), ((), ())), preferred_element_type=jnp.float32)
        activated = jax.nn.gelu(pre_act, approximate=False).astype(jnp.bfloat16)
        branch_out = lax.dot_general(w_out, activated, (((0,), (0,)), ((), ())),
                                     preferred_element_type=jnp.float32).astype(jnp.bfloat16)
        grad_act = jnp.dot(w_out, cotangent, preferred_element_type=jnp.float32)
        grad_pre = (grad_act * gelu_slope(pre_act)).astype(jnp.bfloat16)
        grad_feat = jnp.dot(w_in, grad_pre, preferred_element_type=jnp.float32).astype(jnp.bfloat16)
        sum_in = running[0] + lax.dot_general(features, grad_pre, (((1,), (1,)), ((), ())),
                                              preferred_element_type=jnp.float32)
        sum_out = running[1] + lax.dot_general(activated, cotangent, (((1,), (1,)), ((), ())),
                                               preferred_element_type=jnp.float32)
        return (sum_in, sum_out), (branch_out, grad_feat)

    start_sums = (jnp.zeros((C, HID), jnp.float32), jnp.zeros((HID, C), jnp.float32))
    (sum_in, sum_out), (branch_out, grad_hidden) = lax.scan(per_tile, start_sums, (hidden, grad_out))
    outputs = (inputs.astype(jnp.float32) + branch_out.astype(jnp.float32)).astype(jnp.bfloat16)
    grad_tiles = grad_hidden.reshape(TILES, C, SIDE, SIDE).astype(jnp.float32)
    grad_padded = spread(grad_tiles, kernel, (0, ext_len), (0, ext_len))
    kernel_sum = kernel_grads(grad_tiles, padded, SIDE, (0, 2, 3))
    accum = grad_out.reshape(TILES, C, SIDE, SIDE).astype(jnp.float32)
    accum = accum + grad_padded[:, :, halo_width:halo_width + SIDE, halo_width:halo_width + SIDE]
    for direction, (step_row, step_col) in enumerate(offsets):
        src_rows = source_span(step_row, SIDE, halo_width)
        src_cols = source_span(step_col, SIDE, halo_width)
        dst_rows = target_span(step_row, SIDE, halo_width)
        dst_cols = target_span(step_col, SIDE, halo_width)
        placed = jnp.zeros((TILES, C, SIDE, SIDE), jnp.float32).at[:, :, src_rows[0]:src_rows[1], src_cols[0]:src_cols[1]].set(
            grad_padded[:, :, dst_rows[0]:dst_rows[1], dst_cols[0]:dst_cols[1]])
        back = rotate_tile(placed, (4 - rotations[:, direction]) % 4)
        accum = accum.at[neighbours[:, direction]].add(back)
    grad_in = accum.astype(jnp.bfloat16).reshape(TILES, C, PIX)
    grad_scale = (TILES * PIX) ** -0.5
    return (outputs, grad_in, sum_in * grad_scale, sum_out * grad_scale, kernel_sum * grad_scale)
```

```python
import jax
import jax.numpy as jnp
from jax import lax
from jax.experimental import pallas as pl
from jax.experimental.pallas import tpu as pltpu
from jax.sharding import PartitionSpec as P

NX, NZ, NYL, NYH = 4, 12, 2, 4
NXY = NX * NYL
NY = NYL * NYH
NCHAN = NYH * 2
CH = 32
SIDE = 32
LANES = 128
GROUPS = 8
PADS = SIDE + 4
TAPS = 25
HID = 1024
FULL = 256
SCALE = (NXY * NZ * SIDE * SIDE) ** -0.5
MESH = pl.DeviceIdType.MESH
F32, BF16, I32 = jnp.float32, jnp.bfloat16, jnp.int32

BASE = (0, 0, 0, 3, 1, 2, 2, 2)
EDGE_DIRS = (1, 3, 4, 6)
CORNER_DIRS = (0, 2, 5, 7)

VMEM = pl.BlockSpec(memory_space=pltpu.VMEM)
SMEM = pl.BlockSpec(memory_space=pltpu.SMEM)


def iota(shape, axis):
    return lax.broadcasted_iota(I32, shape, axis)


def roll(values, shift):
    return pltpu.roll(values, shift % LANES, 1)


def dot(a, b, contract=((1,), (0,)), precision=None):
    return lax.dot_general(a, b, (contract, ((), ())), preferred_element_type=F32, precision=precision)


def turned(q, i, j):
    q0, q1, q2, q3 = [(q == k).astype(I32) for k in range(4)]
    rows = q0 * i + q1 * j + q2 * (31 - i) + q3 * (31 - j)
    cols = q0 * j + q1 * (31 - i) + q2 * (31 - j) + q3 * i
    return rows, cols


def fold(wide):
    low = iota((16, LANES), 1) < 64
    return jnp.where(low, wide[:16], roll(wide[16:], 64))


def unfold(tile):
    tile = tile.astype(F32)
    return jnp.concatenate([tile, roll(tile, 64)], axis=0).astype(BF16)


def spread_taps(k_ref, kb):
    taps = k_ref[...].astype(F32)
    eye = iota((CH, CH), 0) == iota((CH, CH), 1)
    ones = jnp.ones((CH, LANES), BF16)
    for tap in range(TAPS):
        row = jnp.broadcast_to(taps[tap : tap + 1, :], (CH, CH))
        kb[tap] = dot(jnp.where(eye, row, 0.0).astype(BF16), ones)


def rim_kernel(x_ref, o_ref):
    p = iota((1024, 256), 0)
    n = iota((1, 256), 1)
    e, line, i = n >> 6, (n >> 5) & 1, n & 31
    px = jnp.where(e == 0, (30 + line) * 32 + i, 0)
    px = jnp.where(e == 1, i * 32 + line, px)
    px = jnp.where(e == 2, line * 32 + i, px)
    px = jnp.where(e == 3, i * 32 + 30 + line, px)
    rims = dot(x_ref[...], jnp.where(p == px, 1.0, 0.0).astype(BF16))
    low = iota((16, LANES), 1) < 64
    for pair in range(2):
        half = rims[:, LANES * pair : LANES * (pair + 1)]
        upper, lower = half[:16], half[16:]
        o_ref[2 * pair] = jnp.where(low, upper, roll(lower, 64)).astype(BF16)
        o_ref[2 * pair + 1] = jnp.where(low, roll(upper, 64), lower).astype(BF16)


def conv_kernel(rot_ref, x_ref, sel_ref, k_ref, hid_ref, pad_ref, pb, kb):
    me = lax.axis_index("tile")
    spread_taps(k_ref, kb)

    def block(d, i, j, valid):
        q = rot_ref[me, d]
        si, sj = turned(q, i, j)
        e = (q + BASE[d]) & 3
        along = (e & 1) * si + (1 - (e & 1)) * sj
        line = (1 - (e & 1)) * (si - 30 * (e == 0).astype(I32)) + (e & 1) * (sj - 30 * (e == 3).astype(I32))
        lane = jnp.where(valid, line * 32 + along, -1)
        pick = jnp.where(iota((LANES, lane.shape[1]), 0) == lane, 1.0, 0.0).astype(BF16)
        return dot(unfold(sel_ref[d]), pick)

    n = iota((1, 256), 1)
    a, lane = n >> 7, n & 127
    rows = []
    for first, dirs in ((30, (0, 1, 2)), (0, (5, 6, 7))):
        i = first + a
        rows.append(
            block(dirs[0], i, 30 + lane, lane < 2)
            + block(dirs[1], i, lane - 2, (lane >= 2) & (lane < 34))
            + block(dirs[2], i, lane - 34, (lane >= 34) & (lane < 36))
        )
    m = iota((1, LANES), 1)
    left = block(3, m >> 1, 30 + (m & 1), m < 64)
    right = block(4, m >> 1, m & 1, m < 64)
    lanes = iota((CH, LANES), 1)

    def put(r, row):
        pad_ref[r] = row.astype(BF16)
        for b in range(5):
            pb[b, r] = roll(row, -b) if b else row

    for k in range(2):
        put(k, rows[0][:, LANES * k : LANES * (k + 1)])
        put(34 + k, rows[1][:, LANES * k : LANES * (k + 1)])
    for g in range(GROUPS):
        chunk = x_ref[:, LANES * g : LANES * (g + 1)].astype(F32)
        for k in range(4):
            r = 4 * g + k
            row = roll(chunk, 2 - 32 * k)
            row = jnp.where(lanes < 2, roll(left, -2 * r), row)
            put(r + 2, jnp.where(lanes >= 34, roll(right, 34 - 2 * r), row))

    def group(g, carry):
        out = jnp.zeros((CH, LANES), F32)
        for k in range(4):
            acc = jnp.zeros((CH, LANES), F32)
            for a in range(5):
                for b in range(5):
                    acc = acc + kb[5 * a + b] * pb[b, 4 * g + k + a]
            out = jnp.where(lanes >> 5 == k, roll(acc, 32 * k), out)
        hid_ref[g] = out.astype(BF16)
        return carry

    lax.fori_loop(0, GROUPS, group, 0)


def dense_kernel(feat_ref, cot_ref, win_ref, wout_ref, br_ref, gf_ref, g_ref):
    feat = feat_ref[...].reshape(FULL, LANES)
    cot = cot_ref[...].reshape(FULL, LANES)
    branch = jnp.zeros((FULL, LANES), F32)
    gfeat = jnp.zeros((FULL, LANES), F32)
    for part in range(4):
        lo = FULL * part
        w_in = win_ref[:, lo : lo + FULL]
        w_out = wout_ref[lo : lo + FULL, :]
        pre = dot(w_in, feat, ((0,), (0,)))
        cumul = 0.5 * (1.0 + lax.erf(pre * 0.7071067811865476))
        act = (pre * cumul).astype(BF16)
        gact = dot(w_out, cot)
        slope = cumul + pre * jnp.exp(-0.5 * pre * pre) * 0.3989422804014327
        gpre = (gact * slope).astype(BF16)
        branch = branch + dot(w_out, act, ((0,), (0,)))
        gfeat = gfeat + dot(w_in, gpre)
        g_ref[lo : lo + FULL, :] = dot(act, cot, ((1,), (1,)))
        g_ref[HID + lo : HID + lo + FULL, :] = dot(feat, gpre, ((1,), (1,)))
    br_ref[...] = branch.astype(BF16).reshape(GROUPS, CH, LANES)
    gf_ref[...] = gfeat.astype(BF16).reshape(GROUPS, CH, LANES)


def back_kernel(x_ref, bo_ref, gh_ref, go_ref, k_ref, pad_ref, out_ref, acc_ref, bt_ref, kg_ref, pb, gb, gp, kb, ka):
    spread_taps(k_ref, kb)
    lanes = iota((CH, LANES), 1)
    zero = jnp.zeros((CH, LANES), F32)
    for r in range(4):
        for b in range(5):
            gb[b, r] = zero
            gb[b, SIDE + 4 + r] = zero
    for g in range(GROUPS):
        span = slice(LANES * g, LANES * (g + 1))
        out_ref[:, span] = (x_ref[:, span].astype(F32) + bo_ref[g].astype(F32)).astype(BF16)
        chunk = gh_ref[g].astype(F32)
        for k in range(4):
            row = jnp.where(lanes < 32, roll(chunk, -32 * k) if k else chunk, 0.0)
            for b in range(5):
                gb[b, 4 * g + k + 4] = roll(row, b) if b else row

    def shift(r, carry):
        row = pad_ref[r].astype(F32)
        for b in range(5):
            pb[b, r] = roll(row, -b) if b else row
        return carry

    lax.fori_loop(0, PADS, shift, 0)

    def spread(q, carry):
        acc = zero
        for a in range(5):
            for b in range(5):
                acc = acc + kb[5 * a + b] * gb[b, q + (4 - a)]
        gp[q] = acc
        return carry

    lax.fori_loop(0, PADS, spread, 0)
    for b in range(5):

        def taps(u, sums, b=b):
            grad = gb[0, u + 4]
            return tuple(sums[a] + grad * pb[b, u + a] for a in range(5))

        sums = lax.fori_loop(0, SIDE, taps, (zero,) * 5)
        for a in range(5):
            ka[5 * a + b] = sums[a]
    for tap in range(TAPS, 28):
        ka[tap] = zero
    totals = dot(jnp.ones((8, LANES), F32), ka[...].reshape(28 * CH, LANES), ((1,), (1,)), lax.Precision.HIGHEST)
    sub = iota((8, LANES), 0)
    kg = jnp.zeros((8, LANES), F32)
    for i in range(7):
        kg = jnp.where(sub == i, totals[:, LANES * i : LANES * (i + 1)], kg)
    kg_ref[...] = kg

    top, left, right, bottom, corners = zero, zero, zero, zero, zero
    for line in range(2):
        upper, lower = gp[line], gp[34 + line]
        top = jnp.where(lanes >> 5 == line, roll(upper, 32 * line - 2), top)
        bottom = jnp.where(lanes >> 5 == line, roll(lower, 32 * line - 2), bottom)
        for i, (row, first) in enumerate(((upper, 0), (upper, 34), (lower, 0), (lower, 34))):
            corners = jnp.where(lanes >> 1 == 2 * i + line, roll(row, 4 * i + 2 * line - first), corners)
    for g in range(GROUPS):
        span = slice(LANES * g, LANES * (g + 1))
        total = zero
        for k in range(4):
            r = 4 * g + k
            row = gp[r + 2]
            left = jnp.where(lanes >> 1 == r, roll(row, 2 * r), left)
            right = jnp.where(lanes >> 1 == r, roll(row, 2 * r - 34), right)
            total = jnp.where(lanes >> 5 == k, roll(row, 32 * k - 2), total)
        acc_ref[g] = total + go_ref[:, span].astype(F32)
    for i, wide in enumerate((top, left, right, bottom, corners)):
        bt_ref[i] = fold(wide).astype(BF16)


def last_kernel(nb_ref, rot_ref, acc_ref, sel_ref, o_ref):
    me = lax.axis_index("tile")
    k = iota((LANES, 1), 0)
    p = iota((1, 1024), 1)
    total = jnp.zeros((CH, 1024), F32)
    for index, d in enumerate(EDGE_DIRS):
        q = rot_ref[nb_ref[me, 7 - d], d]
        line, along = ((k >> 5), (k & 31)) if d in (1, 6) else ((k & 1), (k >> 1))
        edge = line + (30 if d in (1, 3) else 0)
        si, sj = turned(q, edge, along) if d in (1, 6) else turned(q, along, edge)
        place = jnp.where((p == si * 32 + sj) & (k < 64), 1.0, 0.0).astype(BF16)
        total = total + dot(unfold(sel_ref[index]), place)
    q = jnp.zeros((LANES, 1), I32)
    for index, d in enumerate(CORNER_DIRS):
        q = jnp.where(k >> 2 == index, rot_ref[nb_ref[me, 7 - d], d], q)
    i = ((k >> 1) & 1) + jnp.where(k < 8, 30, 0)
    j = (k & 1) + jnp.where((k >> 2) & 1 == 0, 30, 0)
    si, sj = turned(q, i, j)
    place = jnp.where((p == si * 32 + sj) & (k < 16), 1.0, 0.0).astype(BF16)
    total = total + dot(unfold(sel_ref[4]), place)
    for g in range(GROUPS):
        span = slice(LANES * g, LANES * (g + 1))
        o_ref[:, span] = (acc_ref[g] + total[:, span]).astype(BF16)


class Place:
    def __init__(self):
        self.tile, self.chan = lax.axis_index("tile"), lax.axis_index("chan")
        self.z = lax.rem(self.tile, NZ)
        self.xy = lax.div(self.tile, NZ)
        self.x = lax.rem(self.xy, NX)
        self.yl = lax.div(self.xy, NX)
        self.core = lax.rem(self.chan, 2)
        self.yh = lax.div(self.chan, 2)
        self.y = self.yh * NYL + self.yl

    def at(self, tile, chan):
        return {"tile": tile, "chan": chan}

    def along_z(self, k):
        return self.at(self.xy * NZ + lax.rem(self.z + k, NZ), self.chan)

    def tile_xy(self, k):
        return lax.rem(self.xy + k, NXY) * NZ + self.z

    def along_xy(self, k):
        return self.at(self.tile_xy(k), self.chan)

    def along_x(self, k):
        return self.at((self.yl * NX + lax.rem(self.x + k, NX)) * NZ + self.z, self.chan)

    def along_yl(self, k):
        return self.at((lax.rem(self.yl + k, NYL) * NX + self.x) * NZ + self.z, self.chan)

    def along_y(self, k):
        y = lax.rem(self.y + k, NY)
        return self.at((lax.rem(y, NYL) * NX + self.x) * NZ + self.z, lax.div(y, NYL) * 2 + self.core)

    def along_chan(self, k):
        return self.at(self.tile, lax.rem(self.chan + k, NCHAN))

    def partner(self):
        return self.at(self.tile, self.yh * 2 + (1 - self.core))


def meet(devices):
    barrier = pltpu.get_barrier_semaphore()
    for device in devices:
        pl.semaphore_signal(barrier, inc=1, device_id=device, device_id_type=MESH)
    pl.semaphore_wait(barrier, len(devices))


def send(src, dst, sems, k, device):
    copy = pltpu.make_async_remote_copy(
        src_ref=src, dst_ref=dst, send_sem=sems[0].at[k], recv_sem=sems[1].at[k], device_id=device, device_id_type=MESH
    )
    copy.start()
    return copy


def landed(copies):
    for copy in copies:
        copy.wait_recv()


def sent(copies):
    for copy in copies:
        copy.wait_send()


def gather_kernel(nb_ref, rot_ref, rim_ref, go_ref, sel_ref, cot_ref, zbuf, out, got, *sems):
    at = Place()
    z_sems, xy_sems, chan_sems = sems[0:2], sems[2:4], sems[4:6]
    meet(
        [at.along_z(k) for k in range(1, NZ)]
        + [at.along_xy(k) for k in range(1, NXY)]
        + [at.along_chan(k) for k in range(1, NCHAN)]
    )
    along_z = [send(rim_ref, zbuf.at[k], z_sems, k, at.along_z(k)) for k in range(1, NZ)]
    zbuf[0] = rim_ref[...]
    along_chan = []
    for k in range(1, NCHAN):
        chan = lax.rem(at.chan + k, NCHAN)
        chunk = go_ref.at[:, pl.ds(pl.multiple_of(chan * LANES, LANES), LANES)]
        along_chan.append(send(chunk, cot_ref.at[at.chan], chan_sems, k, at.along_chan(k)))
    cot_ref[at.chan] = go_ref[:, pl.ds(pl.multiple_of(at.chan * LANES, LANES), LANES)]
    landed(along_z)
    along_xy = []
    for k in range(NXY):
        tile = at.tile_xy(k)
        for d in range(8):
            source = nb_ref[tile, d]
            slot = lax.rem(at.z - lax.rem(source, NZ) + NZ, NZ)
            edge = (rot_ref[tile, d] + BASE[d]) & 3
            out[k, d] = zbuf[slot, edge]
        if k:
            along_xy.append(send(out.at[k], got.at[k], xy_sems, k, at.along_xy(k)))
    got[0] = out[0]
    landed(along_xy)
    for d in range(8):
        slot = lax.rem(at.xy - lax.div(nb_ref[at.tile, d], NZ) + NXY, NXY)
        sel_ref[d] = got[slot, d]
    landed(along_chan)
    sent(along_z + along_chan + along_xy)


def swap_kernel(count, *refs):
    srcs, dsts, sems = refs[:count], refs[count : 2 * count], refs[2 * count :]
    at = Place()
    meet([at.along_chan(k) for k in range(1, NCHAN)])
    copies = []
    for index in range(count):
        for k in range(1, NCHAN):
            chan = lax.rem(at.chan + k, NCHAN)
            pair = sems[2 * index : 2 * index + 2]
            copies.append(send(srcs[index].at[chan], dsts[index].at[at.chan], pair, k, at.along_chan(k)))
        dsts[index][at.chan] = srcs[index][at.chan]
    landed(copies)
    sent(copies)


def reduce_kernel(
    nb_ref, bt_ref, kg_ref, g_ref, sel_ref, win_ref, wout_ref, kgrad_ref,
    zbuf, out, got, kz, kx, ky, ksum, kall, ra, sa, rb, sb, rc, sc, rd, ey, fx, hc, *sems
):
    at = Place()
    pairs = [sems[2 * i : 2 * i + 2] for i in range(len(sems) // 2)]
    s_hz, s_hxy, s_kz, s_kx, s_ky, s_kc, s_core, s_x, s_y, s_z, s_ay, s_ax, s_ac = pairs
    meet(
        [at.along_z(k) for k in range(1, NZ)]
        + [at.along_xy(k) for k in range(1, NXY)]
        + [at.along_chan(k) for k in range(1, NCHAN)]
        + [at.along_y(k) for k in range(1, NY)]
    )
    copies = []

    def go(*args):
        copies.append(send(*args))
        return copies[-1]

    half = HID
    other = pl.ds(pl.multiple_of((1 - at.core) * half, half), half)
    mine = pl.ds(pl.multiple_of(at.core * half, half), half)
    core = [go(g_ref.at[other], ra, s_core, 0, at.partner())]
    halo_z = [go(bt_ref, zbuf.at[k], s_hz, k, at.along_z(k)) for k in range(1, NZ)]
    grad_z = [go(kg_ref, kz.at[k], s_kz, k, at.along_z(k)) for k in range(1, NZ)]
    zbuf[0] = bt_ref[...]
    landed(core)
    sa[...] = g_ref[mine] + ra[...]
    part_x = half // NX
    sum_x = []
    for k in range(1, NX):
        rows = pl.ds(pl.multiple_of(lax.rem(at.x + k, NX) * part_x, part_x), part_x)
        sum_x.append(go(sa.at[rows], rb.at[k], s_x, k, at.along_x(k)))

    landed(halo_z)
    lane = iota((16, LANES), 1)
    halo_xy = []
    for k in range(NXY):
        tile = at.tile_xy(k)
        packed = jnp.zeros((16, LANES), BF16)
        for i in range(4):
            slot = lax.rem(at.z - lax.rem(nb_ref[tile, 7 - EDGE_DIRS[i]], NZ) + NZ, NZ)
            out[k, i] = zbuf[slot, i]
            slot = lax.rem(at.z - lax.rem(nb_ref[tile, 7 - CORNER_DIRS[i]], NZ) + NZ, NZ)
            packed = jnp.where((lane >> 2) & 15 == i, zbuf[slot, 4], packed)
        out[k, 4] = packed
        if k:
            halo_xy.append(go(out.at[k], got.at[k], s_hxy, k, at.along_xy(k)))
    got[0] = out[0]

    landed(grad_z)
    total = kg_ref[...]
    for k in range(1, NZ):
        total = total + kz[k]
    ksum[0] = total
    grad_x = [go(ksum.at[0], kx.at[k], s_kx, k, at.along_x(k)) for k in range(1, NX)]

    landed(sum_x)
    total = sa[pl.ds(pl.multiple_of(at.x * part_x, part_x), part_x)]
    for k in range(1, NX):
        total = total + rb[k]
    sb[...] = total
    part_y = part_x // NY
    sum_y = []
    for k in range(1, NY):
        rows = pl.ds(pl.multiple_of(lax.rem(at.y + k, NY) * part_y, part_y), part_y)
        sum_y.append(go(sb.at[rows], rc.at[k], s_y, k, at.along_y(k)))

    landed(grad_x)
    total = ksum[0]
    for k in range(1, NX):
        total = total + kx[k]
    ksum[1] = total
    grad_y = [go(ksum.at[1], ky.at[k], s_ky, k, at.along_yl(k)) for k in range(1, NYL)]

    landed(halo_xy)
    packed = jnp.zeros((16, LANES), BF16)
    for i in range(4):
        slot = lax.rem(at.xy - lax.div(nb_ref[at.tile, 7 - EDGE_DIRS[i]], NZ) + NXY, NXY)
        sel_ref[i] = got[slot, i]
        slot = lax.rem(at.xy - lax.div(nb_ref[at.tile, 7 - CORNER_DIRS[i]], NZ) + NXY, NXY)
        packed = jnp.where((lane >> 2) & 15 == i, got[slot, 4], packed)
    sel_ref[4] = packed

    landed(sum_y)
    total = sb[pl.ds(pl.multiple_of(at.y * part_y, part_y), part_y)]
    for k in range(1, NY):
        total = total + rc[k]
    sc[...] = total
    sum_z = [go(sc, rd.at[k], s_z, k, at.along_z(k)) for k in range(1, NZ)]

    landed(grad_y)
    ksum[2] = (ksum[1] + ky[1]) * SCALE
    kall[at.chan] = ksum[2]
    grad_c = [go(ksum.at[2], kall.at[at.chan], s_kc, k, at.along_chan(k)) for k in range(1, NCHAN)]

    landed(sum_z)
    total = sc[...]
    for k in range(1, NZ):
        total = total + rd[k]
    ey[at.y] = (total * SCALE).astype(BF16)
    all_y = [go(ey.at[at.y], ey.at[at.y], s_ay, k, at.along_y(k)) for k in range(1, NY)]

    landed(grad_c)
    low = iota((8, LANES), 1) >> 5
    for j in range(4):
        for side in range(2):
            rows = jnp.zeros((8, LANES), F32)
            for k in range(4):
                rows = jnp.where(low == k, roll(kall[4 * side + k], 32 * (k - j)), rows)
            for i in range(7):
                if 4 * i + j < TAPS:
                    kgrad_ref[4 * i + j : 4 * i + j + 1, LANES * side : LANES * (side + 1)] = rows[i : i + 1]

    landed(all_y)
    for y in range(NY):
        fx[at.x, part_y * y : part_y * (y + 1)] = ey[y]
    all_x = [go(fx.at[at.x], fx.at[at.x], s_ax, k, at.along_x(k)) for k in range(1, NX)]
    landed(all_x)
    all_c = [go(fx, hc, s_ac, 0, at.partner())]

    def place(refs, first):
        for x in range(NX):
            values = refs[x].astype(F32)
            if first:
                wout_ref[part_x * x : part_x * (x + 1), :] = values
            else:
                win_ref[:, part_x * x : part_x * (x + 1)] = values

    @pl.when(at.core == 0)
    def _():
        place(fx, True)

    @pl.when(at.core == 1)
    def _():
        place(fx, False)

    landed(all_c)

    @pl.when(at.core == 0)
    def _():
        place(hc, False)

    @pl.when(at.core == 1)
    def _():
        place(hc, True)

    sent(copies)


def dma(count):
    return [pltpu.SemaphoreType.DMA((count,))] * 2


def call(kernel, outs, ins, scratch=(), smem=0, remote=None, name=None):
    params = {} if remote is None else dict(collective_id=remote, has_side_effects=True)
    return pl.pallas_call(
        kernel,
        out_shape=[jax.ShapeDtypeStruct(shape, dtype) for shape, dtype in outs],
        in_specs=[SMEM] * smem + [VMEM] * (len(ins) - smem),
        out_specs=[VMEM] * len(outs),
        scratch_shapes=list(scratch),
        compiler_params=pltpu.CompilerParams(vmem_limit_bytes=48 << 20, **params),
        name=name,
    )(*ins)


def body(inputs, grad_out, kernel, w_in, w_out, neighbours, rotations):
    x = inputs.reshape(CH, 1024)
    go = grad_out.reshape(CH, 1024)
    chunks = (GROUPS, CH, LANES)
    (rims,) = call(rim_kernel, [((4, 16, LANES), BF16)], [x], name="rims")
    sel, cot = call(
        gather_kernel,
        [((8, 16, LANES), BF16), (chunks, BF16)],
        [neighbours, rotations, rims, go],
        [
            pltpu.VMEM((NZ, 4, 16, LANES), BF16),
            pltpu.VMEM((NXY, 8, 16, LANES), BF16),
            pltpu.VMEM((NXY, 8, 16, LANES), BF16),
            *dma(NZ), *dma(NXY), *dma(NCHAN),
        ],
        smem=2, remote=1, name="halo",
    )
    hid, padded = call(
        conv_kernel,
        [(chunks, BF16), ((PADS, CH, LANES), BF16)],
        [rotations, x, sel, kernel],
        [pltpu.VMEM((5, PADS, CH, LANES), F32), pltpu.VMEM((TAPS, CH, LANES), F32)],
        smem=1, name="conv",
    )
    (feat,) = call(lambda *refs: swap_kernel(1, *refs), [(chunks, BF16)], [hid], dma(NCHAN), remote=2, name="swap1")
    branch, gfeat, grads = call(
        dense_kernel,
        [(chunks, BF16), (chunks, BF16), ((2 * HID, FULL), F32)],
        [feat, cot, w_in, w_out],
        name="dense",
    )
    bo, gh = call(
        lambda *refs: swap_kernel(2, *refs), [(chunks, BF16)] * 2, [branch, gfeat], dma(NCHAN) * 2, remote=3, name="swap2"
    )
    outputs, acc, border, kg = call(
        back_kernel,
        [((CH, 1024), BF16), (chunks, F32), ((5, 16, LANES), BF16), ((8, LANES), F32)],
        [x, bo, gh, go, kernel, padded],
        [
            pltpu.VMEM((5, PADS, CH, LANES), F32),
            pltpu.VMEM((5, SIDE + 8, CH, LANES), F32),
            pltpu.VMEM((PADS, CH, LANES), F32),
            pltpu.VMEM((TAPS, CH, LANES), F32),
            pltpu.VMEM((28, CH, LANES), F32),
        ],
        name="back",
    )
    part_x = HID // NX
    part_y = part_x // NY
    sel2, grad_w_in, grad_w_out, grad_kernel = call(
        reduce_kernel,
        [((5, 16, LANES), BF16), ((FULL, HID), F32), ((HID, FULL), F32), ((TAPS, FULL), F32)],
        [neighbours, border, kg, grads],
        [
            pltpu.VMEM((NZ, 5, 16, LANES), BF16),
            pltpu.VMEM((NXY, 5, 16, LANES), BF16),
            pltpu.VMEM((NXY, 5, 16, LANES), BF16),
            pltpu.VMEM((NZ, 8, LANES), F32),
            pltpu.VMEM((NX, 8, LANES), F32),
            pltpu.VMEM((NYL, 8, LANES), F32),
            pltpu.VMEM((3, 8, LANES), F32),
            pltpu.VMEM((NCHAN, 8, LANES), F32),
            pltpu.VMEM((HID, FULL), F32),
            pltpu.VMEM((HID, FULL), F32),
            pltpu.VMEM((NX, part_x, FULL), F32),
            pltpu.VMEM((part_x, FULL), F32),
            pltpu.VMEM((NY, part_y, FULL), F32),
            pltpu.VMEM((part_y, FULL), F32),
            pltpu.VMEM((NZ, part_y, FULL), F32),
            pltpu.VMEM((NY, part_y, FULL), BF16),
            pltpu.VMEM((NX, part_x, FULL), BF16),
            pltpu.VMEM((NX, part_x, FULL), BF16),
            *dma(NZ), *dma(NXY), *dma(NZ), *dma(NX), *dma(NYL), *dma(NCHAN),
            *dma(1), *dma(NX), *dma(NY), *dma(NZ), *dma(NY), *dma(NX), *dma(1),
        ],
        smem=1, remote=4, name="reduce",
    )
    (grad_in,) = call(last_kernel, [((CH, 1024), BF16)], [neighbours, rotations, acc, sel2], smem=2, name="last")
    return outputs.reshape(1, CH, 1024), grad_in.reshape(1, CH, 1024), grad_w_in, grad_w_out, grad_kernel


def solution(mesh):
    split = P("tile", "chan", None)
    return jax.shard_map(
        body,
        mesh=mesh,
        in_specs=(split, split, P(None, "chan"), P(), P(), P(), P()),
        out_specs=(split, split, P(), P(), P()),
        check_vma=False,
    )
```

```python
import jax
import jax.numpy as jnp
from jax import lax
from jax.experimental import pallas as pl
from jax.experimental.pallas import tpu as pltpu
from jax.sharding import PartitionSpec as P

NX, NZ, NYL, NYH = 4, 12, 2, 4
NXY = NX * NYL
NY = NYL * NYH
NCHAN = NYH * 2
CH = 32
SIDE = 32
LANES = 128
GROUPS = 8
PADS = SIDE + 4
TAPS = 25
HID = 1024
FULL = 256
SCALE = (NXY * NZ * SIDE * SIDE) ** -0.5
MESH = pl.DeviceIdType.MESH
F32, BF16, I32 = jnp.float32, jnp.bfloat16, jnp.int32

BASE = (0, 0, 0, 3, 1, 2, 2, 2)
EDGE_DIRS = (1, 3, 4, 6)
CORNER_DIRS = (0, 2, 5, 7)

VMEM = pl.BlockSpec(memory_space=pltpu.VMEM)
SMEM = pl.BlockSpec(memory_space=pltpu.SMEM)


def iota(shape, axis):
    return lax.broadcasted_iota(I32, shape, axis)


def roll(values, shift):
    return pltpu.roll(values, shift % LANES, 1)


def dot(a, b, contract=((1,), (0,)), precision=None):
    return lax.dot_general(a, b, (contract, ((), ())), preferred_element_type=F32, precision=precision)


def turned(q, i, j):
    q0, q1, q2, q3 = [(q == k).astype(I32) for k in range(4)]
    rows = q0 * i + q1 * j + q2 * (31 - i) + q3 * (31 - j)
    cols = q0 * j + q1 * (31 - i) + q2 * (31 - j) + q3 * i
    return rows, cols


def fold(wide):
    low = iota((16, LANES), 1) < 64
    return jnp.where(low, wide[:16], roll(wide[16:], 64))


def unfold(tile):
    tile = tile.astype(F32)
    return jnp.concatenate([tile, roll(tile, 64)], axis=0).astype(BF16)


def spread_taps(k_ref, kb):
    taps = k_ref[...].astype(F32)
    eye = iota((CH, CH), 0) == iota((CH, CH), 1)
    ones = jnp.ones((CH, LANES), BF16)
    for tap in range(TAPS):
        row = jnp.broadcast_to(taps[tap : tap + 1, :], (CH, CH))
        kb[tap] = dot(jnp.where(eye, row, 0.0).astype(BF16), ones)


def rims_of(x_ref, rim):
    p = iota((1024, 256), 0)
    n = iota((1, 256), 1)
    e, line, i = n >> 6, (n >> 5) & 1, n & 31
    px = jnp.where(e == 0, (30 + line) * 32 + i, 0)
    px = jnp.where(e == 1, i * 32 + line, px)
    px = jnp.where(e == 2, line * 32 + i, px)
    px = jnp.where(e == 3, i * 32 + 30 + line, px)
    rims = dot(x_ref[...], jnp.where(p == px, 1.0, 0.0).astype(BF16))
    low = iota((16, LANES), 1) < 64
    for pair in range(2):
        half = rims[:, LANES * pair : LANES * (pair + 1)]
        upper, lower = half[:16], half[16:]
        rim[2 * pair] = jnp.where(low, upper, roll(lower, 64)).astype(BF16)
        rim[2 * pair + 1] = jnp.where(low, roll(upper, 64), lower).astype(BF16)


def make_picks(rot_ref, me, wide, narrow):
    def pick(d, i, j, valid):
        q = rot_ref[me, d]
        si, sj = turned(q, i, j)
        e = (q + BASE[d]) & 3
        along = (e & 1) * si + (1 - (e & 1)) * sj
        line = (1 - (e & 1)) * (si - 30 * (e == 0).astype(I32)) + (e & 1) * (sj - 30 * (e == 3).astype(I32))
        lane = jnp.where(valid, line * 32 + along, -1)
        return jnp.where(iota((LANES, lane.shape[1]), 0) == lane, 1.0, 0.0).astype(BF16)

    n = iota((1, 2 * LANES), 1)
    a, lane = n >> 7, n & 127
    for side, (first, dirs) in enumerate(((30, (0, 1, 2)), (0, (5, 6, 7)))):
        i = first + a
        wide[3 * side] = pick(dirs[0], i, 30 + lane, lane < 2)
        wide[3 * side + 1] = pick(dirs[1], i, lane - 2, (lane >= 2) & (lane < 34))
        wide[3 * side + 2] = pick(dirs[2], i, lane - 34, (lane >= 34) & (lane < 36))
    m = iota((1, LANES), 1)
    narrow[0] = pick(3, m >> 1, 30 + (m & 1), m < 64)
    narrow[1] = pick(4, m >> 1, m & 1, m < 64)


def make_places(nb_ref, rot_ref, me, places):
    k = iota((LANES, 1), 0)
    p = iota((1, 1024), 1)
    for index, d in enumerate(EDGE_DIRS):
        q = rot_ref[nb_ref[me, 7 - d], d]
        line, along = ((k >> 5), (k & 31)) if d in (1, 6) else ((k & 1), (k >> 1))
        edge = line + (30 if d in (1, 3) else 0)
        si, sj = turned(q, edge, along) if d in (1, 6) else turned(q, along, edge)
        places[index] = jnp.where((p == si * 32 + sj) & (k < 64), 1.0, 0.0).astype(BF16)
    q = jnp.zeros((LANES, 1), I32)
    for index, d in enumerate(CORNER_DIRS):
        q = jnp.where(k >> 2 == index, rot_ref[nb_ref[me, 7 - d], d], q)
    i = ((k >> 1) & 1) + jnp.where(k < 8, 30, 0)
    j = (k & 1) + jnp.where((k >> 2) & 1 == 0, 30, 0)
    si, sj = turned(q, i, j)
    places[4] = jnp.where((p == si * 32 + sj) & (k < 16), 1.0, 0.0).astype(BF16)


def inner_conv(x_ref, kb, pb, part):
    lanes = iota((CH, LANES), 1)
    zero = jnp.zeros((CH, LANES), F32)
    for r in (0, 1, 34, 35):
        for b in range(5):
            pb[b, r] = zero
    for g in range(GROUPS):
        chunk = x_ref[:, LANES * g : LANES * (g + 1)].astype(F32)
        for k in range(4):
            row = jnp.where((lanes >= 2) & (lanes < 34), roll(chunk, 2 - 32 * k), 0.0)
            for b in range(5):
                pb[b, 4 * g + k + 2] = roll(row, -b) if b else row

    def group(g, carry):
        out = zero
        for k in range(4):
            acc = zero
            for a in range(5):
                for b in range(5):
                    acc = acc + kb[5 * a + b] * pb[b, 4 * g + k + a]
            out = jnp.where(lanes >> 5 == k, roll(acc, 32 * k), out)
        part[g] = out
        return carry

    lax.fori_loop(0, GROUPS, group, 0)


def outer_conv(tiles, wide, narrow, kb, part, rows_ref, cols_ref, hid):
    lanes = iota((CH, LANES), 1)
    zero = jnp.zeros((CH, LANES), F32)
    above = dot(tiles[0], wide[0]) + dot(tiles[1], wide[1]) + dot(tiles[2], wide[2])
    below = dot(tiles[5], wide[3]) + dot(tiles[6], wide[4]) + dot(tiles[7], wide[5])
    left, right = dot(tiles[3], narrow[0]), dot(tiles[4], narrow[1])
    rows = (above[:, :LANES], above[:, LANES:], below[:, :LANES], below[:, LANES:])
    for i in range(4):
        rows_ref[i] = rows[i]
    cols_ref[0], cols_ref[1] = left, right
    first, second, last, prior = zero, zero, zero, zero
    for b in range(5):
        r0, r1, r2, r3 = [roll(row, -b) if b else row for row in rows]
        first = first + kb[b] * r0 + kb[5 + b] * r1
        second = second + kb[b] * r1
        prior = prior + kb[20 + b] * r2
        last = last + kb[15 + b] * r2 + kb[20 + b] * r3
    even = lanes & 1 == 0
    low, high = zero, zero
    for a in range(5):
        one = roll(left, -2 * (a - 2))
        low = low + kb[5 * a] * one + jnp.where(even, kb[5 * a + 1] * roll(one, -1), 0.0)
        one = roll(right, -2 * (a - 2))
        high = high + kb[5 * a + 4] * one + jnp.where(even, 0.0, kb[5 * a + 3] * roll(one, 1))
    for g in range(GROUPS):
        extra = zero
        for k in range(4):
            u = 4 * g + k
            extra = jnp.where(lanes >> 1 == 16 * k, roll(low, 32 * k - 2 * u), extra)
            extra = jnp.where(lanes >> 1 == 16 * k + 15, roll(high, 32 * k + 30 - 2 * u), extra)
        total = part[g] + extra
        if g == 0:
            total = total + jnp.where(lanes < 32, first, jnp.where(lanes < 64, roll(second, 32), 0.0))
        if g == GROUPS - 1:
            total = total + jnp.where(lanes >= 96, roll(last, 96), jnp.where(lanes >= 64, roll(prior, 64), 0.0))
        hid[g] = total.astype(BF16)


def complete_rows(rows_ref, cols_ref, pb):
    lanes = iota((CH, LANES), 1)
    left, right = cols_ref[0], cols_ref[1]
    for i, r in enumerate((0, 1, 34, 35)):
        for b in range(5):
            pb[b, r] = roll(rows_ref[i], -b) if b else rows_ref[i]
    for r in range(SIDE):
        row = jnp.where(lanes < 2, roll(left, -2 * r), pb[0, r + 2])
        row = jnp.where(lanes >> 1 == 17, roll(right, 34 - 2 * r), row)
        for b in range(5):
            pb[b, r + 2] = roll(row, -b) if b else row


def outer_spread(gh, kb, border):
    lanes = iota((CH, LANES), 1)
    zero = jnp.zeros((CH, LANES), F32)
    own = lanes < 32
    first, last = gh[0].astype(F32), gh[GROUPS - 1].astype(F32)
    r0, r1 = jnp.where(own, first, 0.0), jnp.where(own, roll(first, -32), 0.0)
    r30, r31 = jnp.where(own, roll(last, -64), 0.0), jnp.where(own, roll(last, -96), 0.0)
    gp = [zero] * 4
    for b in range(5):
        s0, s1, s30, s31 = [roll(row, b) if b else row for row in (r0, r1, r30, r31)]
        gp[0] = gp[0] + kb[b] * s0
        gp[1] = gp[1] + kb[b] * s1 + kb[5 + b] * s0
        gp[2] = gp[2] + kb[15 + b] * s31 + kb[20 + b] * s30
        gp[3] = gp[3] + kb[20 + b] * s31
    head, tail = zero, zero
    for g in range(GROUPS):
        chunk = gh[g].astype(F32)
        for k in range(4):
            r = 4 * g + k
            head = jnp.where(lanes >> 1 == r, roll(chunk, 2 * r - 32 * k), head)
            tail = jnp.where(lanes >> 1 == r, roll(chunk, 2 * r - 32 * k - 30), tail)
    even = lanes & 1 == 0
    left, right = zero, zero
    for a in range(5):
        one = roll(head, 2 * (a - 2))
        left = left + kb[5 * a] * one + jnp.where(even, 0.0, kb[5 * a + 1] * roll(one, 1))
        one = roll(tail, 2 * (a - 2))
        right = right + kb[5 * a + 4] * one + jnp.where(even, kb[5 * a + 3] * roll(one, -1), 0.0)
    top, bottom, corners = zero, zero, zero
    for line in range(2):
        upper, lower = gp[line], gp[2 + line]
        top = jnp.where(lanes >> 5 == line, roll(upper, 32 * line - 2), top)
        bottom = jnp.where(lanes >> 5 == line, roll(lower, 32 * line - 2), bottom)
        for i, (row, start) in enumerate(((upper, 0), (upper, 34), (lower, 0), (lower, 34))):
            corners = jnp.where(lanes >> 1 == 2 * i + line, roll(row, 4 * i + 2 * line - start), corners)
    for i, wide in enumerate((top, left, right, bottom, corners)):
        border[i] = fold(wide).astype(BF16)


def inner_spread(gh, go_ref, kb, gb, acc_ref):
    lanes = iota((CH, LANES), 1)
    zero = jnp.zeros((CH, LANES), F32)
    for r in (0, 1, 34, 35):
        for b in range(5):
            gb[b, r] = zero
    for g in range(GROUPS):
        chunk = gh[g].astype(F32)
        for k in range(4):
            row = jnp.where(lanes < 32, roll(chunk, -32 * k) if k else chunk, 0.0)
            for b in range(5):
                gb[b, 4 * g + k + 2] = row if b == 2 else roll(row, b - 2)
        acc_ref[g] = go_ref[:, LANES * g : LANES * (g + 1)].astype(F32)

    def group(g, carry):
        out = zero
        for k in range(4):
            acc = zero
            for a in range(5):
                for b in range(5):
                    acc = acc + kb[5 * a + b] * gb[b, 4 * g + (k + 4 - a)]
            out = jnp.where(lanes >> 5 == k, roll(acc, 32 * k), out)
        acc_ref[g] = acc_ref[g] + out
        return carry

    lax.fori_loop(0, GROUPS, group, 0)


def tap_sums(pb, gb, ka):
    zero = jnp.zeros((CH, LANES), F32)
    for b in range(5):

        def taps(u, sums, b=b):
            grad = gb[2, u + 2]
            return tuple(sums[a] + grad * pb[b, u + a] for a in range(5))

        sums = lax.fori_loop(0, SIDE, taps, (zero,) * 5)
        for a in range(5):
            ka[5 * a + b] = sums[a]
    for tap in range(TAPS, 28):
        ka[tap] = zero
    totals = dot(jnp.ones((8, LANES), F32), ka[...].reshape(28 * CH, LANES), ((1,), (1,)), lax.Precision.HIGHEST)
    sub = iota((8, LANES), 0)
    out = jnp.zeros((8, LANES), F32)
    for i in range(7):
        out = jnp.where(sub == i, totals[:, LANES * i : LANES * (i + 1)], out)
    return out


class Place:
    def __init__(self):
        self.tile, self.chan = lax.axis_index("tile"), lax.axis_index("chan")
        self.z = lax.rem(self.tile, NZ)
        self.xy = lax.div(self.tile, NZ)
        self.x = lax.rem(self.xy, NX)
        self.yl = lax.div(self.xy, NX)
        self.core = lax.rem(self.chan, 2)
        self.yh = lax.div(self.chan, 2)
        self.y = self.yh * NYL + self.yl

    def at(self, tile, chan):
        return {"tile": tile, "chan": chan}

    def along_z(self, k):
        return self.at(self.xy * NZ + lax.rem(self.z + k, NZ), self.chan)

    def tile_xy(self, k):
        return lax.rem(self.xy + k, NXY) * NZ + self.z

    def along_xy(self, k):
        return self.at(self.tile_xy(k), self.chan)

    def along_x(self, k):
        return self.at((self.yl * NX + lax.rem(self.x + k, NX)) * NZ + self.z, self.chan)

    def along_yl(self, k):
        return self.at((lax.rem(self.yl + k, NYL) * NX + self.x) * NZ + self.z, self.chan)

    def along_y(self, k):
        y = lax.rem(self.y + k, NY)
        return self.at((lax.rem(y, NYL) * NX + self.x) * NZ + self.z, lax.div(y, NYL) * 2 + self.core)

    def along_chan(self, k):
        return self.at(self.tile, lax.rem(self.chan + k, NCHAN))

    def partner(self):
        return self.at(self.tile, self.yh * 2 + (1 - self.core))


def send(src, dst, sems, k, device):
    copy = pltpu.make_async_remote_copy(
        src_ref=src, dst_ref=dst, send_sem=sems[0].at[k], recv_sem=sems[1].at[k], device_id=device, device_id_type=MESH
    )
    copy.start()
    return copy


def landed(copies):
    for copy in copies:
        copy.wait_recv()


BLOCK = 32
NEAR = (1, 7, 2, 6, 3, 5, 4)
FAR = (4, 3, 5, 2, 6, 1, 7, 0)


def scratch_shapes():
    rows, tile = (CH, LANES), (16, LANES)
    vmem = dict(
        x=((CH, 1024), BF16), go=((CH, 1024), BF16), taps=((TAPS, CH), BF16), win=((FULL, HID), BF16), wout=((HID, FULL), BF16),
        rim=((4, *tile), BF16), zbuf=((NZ, 4, *tile), BF16), xout=((NXY, 8, *tile), BF16), xgot=((NXY, 8, *tile), BF16),
        wide=((6, LANES, 2 * LANES), BF16), narrow=((2, LANES, LANES), BF16), places=((5, LANES, 1024), BF16),
        kb=((TAPS, *rows), F32), pb=((5, PADS, *rows), F32), gb=((5, PADS, *rows), F32), ka=((28, *rows), F32),
        part=((GROUPS, *rows), F32), rows=((4, *rows), F32), cols=((2, *rows), F32), acc=((GROUPS, *rows), F32),
        hid=((GROUPS, *rows), BF16), feat=((GROUPS, *rows), BF16), cot=((GROUPS, *rows), BF16),
        br=((GROUPS, *rows), BF16), gf=((GROUPS, *rows), BF16), bo=((GROUPS, *rows), BF16), gh=((GROUPS, *rows), BF16),
        border=((5, *tile), BF16), bz=((NZ, 5, *tile), BF16), bout=((NXY, 5, *tile), BF16), bgot=((NXY, 5, *tile), BF16),
        kown=((3, 8, LANES), F32), kz=((NZ, 8, LANES), F32), kxy=((NXY, 8, LANES), F32),
        grads=((2, NX, FULL, FULL), F32), terms=((2, NX, FULL, FULL), BF16), rcore=((NX, FULL, FULL), BF16),
        sx=((FULL, FULL), F32), tx=((NX, FULL, FULL), BF16), rx=((NX, NY, BLOCK, FULL), BF16),
        sy=((BLOCK, FULL), F32), ty=((NY, BLOCK, FULL), BF16), ry=((NY, BLOCK, FULL), BF16),
        tz=((BLOCK, FULL), BF16), rz=((NZ, BLOCK, FULL), BF16),
    )
    sems = dict(
        z=NZ, cot=NCHAN, xy=NXY, s1=NCHAN, s2a=NCHAN, s2b=NCHAN, core=NX, x=NX * NY, y=NY, sz=NZ, bz=NZ, bxy=NXY,
        kz=NZ, kxy=NXY, kc=NCHAN, ay=NY, ax=NX * NY, ac=NX * NY,
    )
    return vmem, sems


class Names:
    pass


def step_kernel(
    nb_hbm, rot_hbm, x_hbm, go_hbm, k_hbm, win_hbm, wout_hbm, out_ref, gin_ref, all_ref, kall_ref, load_sem, nb_ref, rot_ref, *rest
):
    vmem, semaphores = scratch_shapes()
    s, sem = Names(), Names()
    for name, ref in zip(vmem, rest):
        setattr(s, name, ref)
    rest = rest[len(vmem) :]
    for index, name in enumerate(semaphores):
        setattr(sem, name, rest[2 * index : 2 * index + 2])
    at = Place()
    copies = []

    def go(*args):
        copies.append(send(*args))
        return copies[-1]

    barrier = pltpu.get_barrier_semaphore()
    peers = (
        [at.along_z(k) for k in range(1, NZ)]
        + [at.along_xy(k) for k in range(1, NXY)]
        + [at.along_chan(k) for k in range(1, NCHAN)]
        + [at.along_y(k) for k in range(1, NY)]
    )
    for device in peers:
        pl.semaphore_signal(barrier, inc=1, device_id=device, device_id_type=MESH)
    pairs = ((x_hbm, s.x), (go_hbm, s.go), (k_hbm, s.taps), (win_hbm, s.win), (wout_hbm, s.wout), (nb_hbm, nb_ref), (rot_hbm, rot_ref))
    loads = [pltpu.make_async_copy(src, dst, load_sem.at[i]) for i, (src, dst) in enumerate(pairs)]
    for load in loads:
        load.start()
    loads[0].wait()
    rims_of(s.x, s.rim)
    loads[1].wait()
    pl.semaphore_wait(barrier, len(peers))

    z_in = [go(s.rim, s.zbuf.at[k], sem.z, k, at.along_z(k)) for k in (6, 5, 7, 4, 8, 3, 9, 2, 10, 1, 11)]
    s.zbuf[0] = s.rim[...]
    cot_in = []
    for k in range(1, NCHAN):
        chan = lax.rem(at.chan + k, NCHAN)
        chunk = s.go.at[:, pl.ds(pl.multiple_of(chan * LANES, LANES), LANES)]
        cot_in.append(go(chunk, s.cot.at[at.chan], sem.cot, k, at.along_chan(k)))
    s.cot[at.chan] = s.go[:, pl.ds(pl.multiple_of(at.chan * LANES, LANES), LANES)]
    loads[2].wait()
    spread_taps(s.taps, s.kb)
    inner_conv(s.x, s.kb, s.pb, s.part)
    loads[5].wait()
    loads[6].wait()
    make_picks(rot_ref, at.tile, s.wide, s.narrow)
    landed(z_in)
    xy_in = []
    for k in (6, 2, 5, 7, 1, 3, 4, 0):
        tile = at.tile_xy(k)
        for d in range(8):
            slot = lax.rem(at.z - lax.rem(nb_ref[tile, d], NZ) + NZ, NZ)
            s.xout[k, d] = s.zbuf[slot, (rot_ref[tile, d] + BASE[d]) & 3]
        if k:
            xy_in.append(go(s.xout.at[k], s.xgot.at[k], sem.xy, k, at.along_xy(k)))
    s.xgot[0] = s.xout[0]
    make_places(nb_ref, rot_ref, at.tile, s.places)
    loads[3].wait()
    loads[4].wait()
    landed(xy_in)
    tiles = []
    for d in range(8):
        slot = lax.rem(at.xy - lax.div(nb_ref[at.tile, d], NZ) + NXY, NXY)
        tiles.append(unfold(s.xgot[slot, d]))
    outer_conv(tiles, s.wide, s.narrow, s.kb, s.part, s.rows, s.cols, s.hid)

    def swap(src, dst, sems):
        moved = []
        for k in (4, 5, 3, 6, 2, 7, 1):
            chan = lax.rem(at.chan + k, NCHAN)
            moved.append(go(src.at[chan], dst.at[at.chan], sems, k, at.along_chan(k)))
        dst[at.chan] = src[at.chan]
        return moved

    feat_in = swap(s.hid, s.feat, sem.s1)
    complete_rows(s.rows, s.cols, s.pb)
    landed(cot_in)
    landed(feat_in)

    feat = s.feat[...].reshape(FULL, LANES)
    cot = s.cot[...].reshape(FULL, LANES)
    branch = jnp.zeros((FULL, LANES), F32)
    gfeat = jnp.zeros((FULL, LANES), F32)
    core_in = []
    for part in range(NX):
        lo = FULL * part
        w_in = s.win[:, lo : lo + FULL]
        w_out = s.wout[lo : lo + FULL, :]
        pre = dot(w_in, feat, ((0,), (0,)))
        cumul = 0.5 * (1.0 + lax.erf(pre * 0.7071067811865476))
        act = (pre * cumul).astype(BF16)
        gact = dot(w_out, cot)
        slope = cumul + pre * jnp.exp(-0.5 * pre * pre) * 0.3989422804014327
        gpre = (gact * slope).astype(BF16)
        branch = branch + dot(w_out, act, ((0,), (0,)))
        gfeat = gfeat + dot(w_in, gpre)
        for side, value in enumerate((dot(act, cot, ((1,), (1,))), dot(feat, gpre, ((1,), (1,))))):
            s.grads[side, part] = value
            s.terms[side, part] = value.astype(BF16)
    s.br[...] = branch.astype(BF16).reshape(GROUPS, CH, LANES)
    s.gf[...] = gfeat.astype(BF16).reshape(GROUPS, CH, LANES)
    grad_in = swap(s.gf, s.gh, sem.s2a)
    for part in range(NX):
        core_in.append(go(s.terms.at[1 - at.core, part], s.rcore.at[part], sem.core, part, at.partner()))
    branch_in = swap(s.br, s.bo, sem.s2b)

    landed(core_in)
    x_in = {}
    for k in (2, 1, 3, 0):
        part = lax.rem(at.x + k, NX)
        total = s.grads[at.core, part] + s.rcore[part].astype(F32)
        if k == 0:
            s.sx[...] = total
            continue
        s.tx[k] = total.astype(BF16)
        for step in FAR:
            rows = pl.ds(pl.multiple_of(lax.rem(at.y + step, NY) * BLOCK, BLOCK), BLOCK)
            x_in[k, step] = go(s.tx.at[k, rows], s.rx.at[k, step], sem.x, k * NY + step, at.along_x(k))

    landed(grad_in)
    outer_spread(s.gh, s.kb, s.border)
    border_in = [go(s.border, s.bz.at[k], sem.bz, k, at.along_z(k)) for k in (6, 5, 7, 4, 8, 3, 9, 2, 10, 1, 11)]
    s.bz[0] = s.border[...]
    inner_spread(s.gh, s.go, s.kb, s.gb, s.acc)

    y_in = {}
    for step in FAR:
        landed([x_in[k, step] for k in (1, 3, 2)])
        total = s.sx[pl.ds(pl.multiple_of(lax.rem(at.y + step, NY) * BLOCK, BLOCK), BLOCK)]
        for k in range(1, NX):
            total = total + s.rx[k, step].astype(F32)
        if step == 0:
            s.sy[...] = total
            continue
        s.ty[step] = total.astype(BF16)
        y_in[step] = go(s.ty.at[step], s.ry.at[step], sem.y, step, at.along_y(step))

    s.kown[0] = tap_sums(s.pb, s.gb, s.ka)
    taps_z = [go(s.kown.at[0], s.kz.at[k], sem.kz, k, at.along_z(k)) for k in range(1, NZ)]

    landed([y_in[step] for step in NEAR])
    total = s.sy[...]
    for step in range(1, NY):
        total = total + s.ry[step].astype(F32)
    s.sy[...] = total
    s.tz[...] = total.astype(BF16)
    sum_z = [go(s.tz, s.rz.at[k], sem.sz, k, at.along_z(k)) for k in (6, 5, 7, 4, 8, 3, 9, 2, 10, 1, 11)]

    landed(border_in)
    lane = iota((16, LANES), 1)
    border_xy = []
    for k in (6, 2, 5, 7, 1, 3, 4, 0):
        tile = at.tile_xy(k)
        packed = jnp.zeros((16, LANES), BF16)
        for i in range(4):
            slot = lax.rem(at.z - lax.rem(nb_ref[tile, 7 - EDGE_DIRS[i]], NZ) + NZ, NZ)
            s.bout[k, i] = s.bz[slot, i]
            slot = lax.rem(at.z - lax.rem(nb_ref[tile, 7 - CORNER_DIRS[i]], NZ) + NZ, NZ)
            packed = jnp.where((lane >> 2) & 15 == i, s.bz[slot, 4], packed)
        s.bout[k, 4] = packed
        if k:
            border_xy.append(go(s.bout.at[k], s.bgot.at[k], sem.bxy, k, at.along_xy(k)))
    s.bgot[0] = s.bout[0]

    landed(taps_z)
    total = s.kown[0]
    for k in range(1, NZ):
        total = total + s.kz[k]
    s.kown[1] = total
    taps_xy = [go(s.kown.at[1], s.kxy.at[k], sem.kxy, k, at.along_xy(k)) for k in range(1, NXY)]

    landed(sum_z)
    total = s.sy[...]
    for k in range(1, NZ):
        total = total + s.rz[k].astype(F32)
    all_ref[at.core, at.x, at.y] = (total * SCALE).astype(BF16)
    own = all_ref.at[at.core, at.x, at.y]
    y_all = {k: go(own, own, sem.ay, k, at.along_y(k)) for k in (4, 3, 5, 2, 6, 1, 7)}
    x_all, core_all = {}, []

    def onward(step):
        block = all_ref.at[at.core, at.x, lax.rem(at.y - step + NY, NY)]
        for k in (2, 1, 3):
            x_all[k, step] = go(block, block, sem.ax, k * NY + step, at.along_x(k))
        core_all.append(go(block, block, sem.ac, step, at.partner()))

    onward(0)

    landed(taps_xy)
    total = s.kown[1]
    for k in range(1, NXY):
        total = total + s.kxy[k]
    s.kown[2] = total * SCALE
    kall_ref[at.chan] = s.kown[2]
    taps_all = [go(s.kown.at[2], kall_ref.at[at.chan], sem.kc, k, at.along_chan(k)) for k in range(1, NCHAN)]

    for step in NEAR:
        landed([y_all[step]])
        onward(step)

    landed(branch_in)
    for g in range(GROUPS):
        span = slice(LANES * g, LANES * (g + 1))
        out_ref[:, span] = (s.x[:, span].astype(F32) + s.bo[g].astype(F32)).astype(BF16)
    landed(border_xy)
    packed = jnp.zeros((16, LANES), BF16)
    total = jnp.zeros((CH, 1024), F32)
    for i in range(4):
        slot = lax.rem(at.xy - lax.div(nb_ref[at.tile, 7 - EDGE_DIRS[i]], NZ) + NXY, NXY)
        total = total + dot(unfold(s.bgot[slot, i]), s.places[i])
        slot = lax.rem(at.xy - lax.div(nb_ref[at.tile, 7 - CORNER_DIRS[i]], NZ) + NXY, NXY)
        packed = jnp.where((lane >> 2) & 15 == i, s.bgot[slot, 4], packed)
    total = total + dot(unfold(packed), s.places[4])
    for g in range(GROUPS):
        span = slice(LANES * g, LANES * (g + 1))
        gin_ref[:, span] = (s.acc[g] + total[:, span]).astype(BF16)

    for step in (0, *NEAR):
        for k in (1, 3, 2):
            landed([x_all[k, step]])
            block = all_ref.at[at.core, lax.rem(at.x - k + NX, NX), lax.rem(at.y - step + NY, NY)]
            core_all.append(go(block, block, sem.ac, k * NY + step, at.partner()))
    landed(taps_all)
    landed(core_all)
    for copy in copies:
        copy.wait_send()


def last_kernel(out_ref, gin_ref, all_ref, kall_ref, out2_ref, gin2_ref, win_ref, wout_ref, kgrad_ref):
    out2_ref[...] = out_ref[...]
    gin2_ref[...] = gin_ref[...]
    for x in range(NX):
        for y in range(NY):
            row = FULL * x + BLOCK * y
            wout_ref[row : row + BLOCK, :] = all_ref[0, x, y].astype(F32)
            win_ref[BLOCK * y : BLOCK * (y + 1), FULL * x : FULL * (x + 1)] = all_ref[1, x, y].astype(F32)
    low = iota((8, LANES), 1) >> 5
    for j in range(4):
        for side in range(2):
            rows = jnp.zeros((8, LANES), F32)
            for k in range(4):
                rows = jnp.where(low == k, roll(kall_ref[4 * side + k], 32 * (k - j)), rows)
            for i in range(7):
                if 4 * i + j < TAPS:
                    kgrad_ref[4 * i + j : 4 * i + j + 1, LANES * side : LANES * (side + 1)] = rows[i : i + 1]


def body(inputs, grad_out, kernel, w_in, w_out, neighbours, rotations):
    vmem, semaphores = scratch_shapes()
    tables = [pltpu.SMEM((NXY * NZ, 8), I32)] * 2
    scratch = [pltpu.SemaphoreType.DMA((7,)), *tables] + [pltpu.VMEM(shape, dtype) for shape, dtype in vmem.values()]
    for count in semaphores.values():
        scratch += [pltpu.SemaphoreType.DMA((count,))] * 2
    shapes = [((CH, 1024), BF16), ((CH, 1024), BF16), ((2, NX, NY, BLOCK, FULL), BF16), ((NCHAN, 8, LANES), F32)]
    results = pl.pallas_call(
        step_kernel,
        out_shape=[jax.ShapeDtypeStruct(shape, dtype) for shape, dtype in shapes],
        in_specs=[pl.BlockSpec(memory_space=pltpu.HBM)] * 7,
        out_specs=[VMEM] * 4,
        scratch_shapes=scratch,
        compiler_params=pltpu.CompilerParams(vmem_limit_bytes=50 << 20, collective_id=1, has_side_effects=True),
        name="step",
    )(neighbours, rotations, inputs.reshape(CH, 1024), grad_out.reshape(CH, 1024), kernel, w_in, w_out)
    shapes = [((CH, 1024), BF16), ((CH, 1024), BF16), ((FULL, HID), F32), ((HID, FULL), F32), ((TAPS, FULL), F32)]
    outputs, grad_in, grad_w_in, grad_w_out, grad_kernel = pl.pallas_call(
        last_kernel,
        out_shape=[jax.ShapeDtypeStruct(shape, dtype) for shape, dtype in shapes],
        in_specs=[VMEM] * 4,
        out_specs=[VMEM] * 5,
        compiler_params=pltpu.CompilerParams(vmem_limit_bytes=12 << 20),
        name="last",
    )(*results)
    return outputs.reshape(1, CH, 1024), grad_in.reshape(1, CH, 1024), grad_w_in, grad_w_out, grad_kernel


def solution(mesh):
    split = P("tile", "chan", None)
    return jax.shard_map(
        body,
        mesh=mesh,
        in_specs=(split, split, P(None, "chan"), P(), P(), P(), P()),
        out_specs=(split, split, P(), P(), P()),
        check_vma=False,
    )
```

```python
import jax
import jax.numpy as jnp
from jax import lax
from jax.experimental import pallas as pl
from jax.experimental.pallas import tpu as pltpu
from jax.sharding import PartitionSpec as P

NX, NZ, NYL, NYH = 4, 12, 2, 4
NXY = NX * NYL
NY = NYL * NYH
NCHAN = NYH * 2
CH = 32
SIDE = 32
LANES = 128
GROUPS = 8
PADS = SIDE + 4
TAPS = 25
HID = 1024
FULL = 256
SCALE = (NXY * NZ * SIDE * SIDE) ** -0.5
MESH = pl.DeviceIdType.MESH
F32, BF16, I32 = jnp.float32, jnp.bfloat16, jnp.int32

BASE = (0, 0, 0, 3, 1, 2, 2, 2)
EDGE_DIRS = (1, 3, 4, 6)
CORNER_DIRS = (0, 2, 5, 7)

VMEM = pl.BlockSpec(memory_space=pltpu.VMEM)
SMEM = pl.BlockSpec(memory_space=pltpu.SMEM)


def iota(shape, axis):
    return lax.broadcasted_iota(I32, shape, axis)


def roll(values, shift):
    return pltpu.roll(values, shift % LANES, 1)


def dot(a, b, contract=((1,), (0,)), precision=None):
    return lax.dot_general(a, b, (contract, ((), ())), preferred_element_type=F32, precision=precision)


def turned(q, i, j):
    q0, q1, q2, q3 = [(q == k).astype(I32) for k in range(4)]
    rows = q0 * i + q1 * j + q2 * (31 - i) + q3 * (31 - j)
    cols = q0 * j + q1 * (31 - i) + q2 * (31 - j) + q3 * i
    return rows, cols


def fold(wide):
    low = iota((16, LANES), 1) < 64
    return jnp.where(low, wide[:16], roll(wide[16:], 64))


def unfold(tile):
    return jnp.concatenate([tile, roll(tile, 64)], axis=0).astype(BF16)


def spread_taps(k_ref, kb):
    taps = k_ref[...].astype(F32)
    eye = iota((CH, CH), 0) == iota((CH, CH), 1)
    ones = jnp.ones((CH, LANES), BF16)
    for tap in range(TAPS):
        row = jnp.broadcast_to(taps[tap : tap + 1, :], (CH, CH))
        kb[tap] = dot(jnp.where(eye, row, 0.0).astype(BF16), ones)


def rims_of(x_ref, rim):
    p = iota((1024, 256), 0)
    n = iota((1, 256), 1)
    e, line, i = n >> 6, (n >> 5) & 1, n & 31
    px = jnp.where(e == 0, (30 + line) * 32 + i, 0)
    px = jnp.where(e == 1, i * 32 + line, px)
    px = jnp.where(e == 2, line * 32 + i, px)
    px = jnp.where(e == 3, i * 32 + 30 + line, px)
    rims = dot(x_ref[...], jnp.where(p == px, 1.0, 0.0).astype(BF16))
    low = iota((16, LANES), 1) < 64
    for pair in range(2):
        half = rims[:, LANES * pair : LANES * (pair + 1)]
        upper, lower = half[:16], half[16:]
        rim[2 * pair] = jnp.where(low, upper, roll(lower, 64)).astype(BF16)
        rim[2 * pair + 1] = jnp.where(low, roll(upper, 64), lower).astype(BF16)


def make_picks(rot_ref, me, wide, narrow):
    def pick(d, i, j, valid):
        q = rot_ref[d, me]
        si, sj = turned(q, i, j)
        e = (q + BASE[d]) & 3
        along = (e & 1) * si + (1 - (e & 1)) * sj
        line = (1 - (e & 1)) * (si - 30 * (e == 0).astype(I32)) + (e & 1) * (sj - 30 * (e == 3).astype(I32))
        lane = jnp.where(valid, line * 32 + along, -1)
        return jnp.where(iota((LANES, lane.shape[1]), 0) == lane, 1.0, 0.0).astype(BF16)

    n = iota((1, 2 * LANES), 1)
    a, lane = n >> 7, n & 127
    for side, (first, dirs) in enumerate(((30, (0, 1, 2)), (0, (5, 6, 7)))):
        i = first + a
        wide[3 * side] = pick(dirs[0], i, 30 + lane, lane < 2)
        wide[3 * side + 1] = pick(dirs[1], i, lane - 2, (lane >= 2) & (lane < 34))
        wide[3 * side + 2] = pick(dirs[2], i, lane - 34, (lane >= 34) & (lane < 36))
    m = iota((1, LANES), 1)
    narrow[0] = pick(3, m >> 1, 30 + (m & 1), m < 64)
    narrow[1] = pick(4, m >> 1, m & 1, m < 64)


def make_places(nb_ref, rot_ref, me, places):
    k = iota((LANES, 1), 0)
    p = iota((1, 1024), 1)
    m = k & 63
    pixels = []
    for d in EDGE_DIRS:
        q = rot_ref[d, nb_ref[7 - d, me]]
        line, along = ((m >> 5), (m & 31)) if d in (1, 6) else ((m & 1), (m >> 1))
        edge = line + (30 if d in (1, 3) else 0)
        si, sj = turned(q, edge, along) if d in (1, 6) else turned(q, along, edge)
        pixels.append(si * 32 + sj)
    for pair in range(2):
        places[pair] = jnp.where(p == jnp.where(k < 64, pixels[2 * pair], pixels[2 * pair + 1]), 1.0, 0.0).astype(BF16)
    q = jnp.zeros((LANES, 1), I32)
    for index, d in enumerate(CORNER_DIRS):
        q = jnp.where(k >> 2 == index, rot_ref[d, nb_ref[7 - d, me]], q)
    i = ((k >> 1) & 1) + jnp.where(k < 8, 30, 0)
    j = (k & 1) + jnp.where((k >> 2) & 1 == 0, 30, 0)
    si, sj = turned(q, i, j)
    places[2] = jnp.where((p == si * 32 + sj) & (k < 16), 1.0, 0.0).astype(BF16)


def inner_conv(x_ref, kb, pb, part):
    lanes = iota((CH, LANES), 1)
    zero = jnp.zeros((CH, LANES), F32)
    for r in (0, 1, 34, 35):
        for b in range(5):
            pb[b, r] = zero
    for g in range(GROUPS):
        chunk = x_ref[:, LANES * g : LANES * (g + 1)].astype(F32)
        for k in range(4):
            row = jnp.where((lanes >= 2) & (lanes < 34), roll(chunk, 2 - 32 * k), 0.0)
            for b in range(5):
                pb[b, 4 * g + k + 2] = roll(row, -b) if b else row

    def group(g, carry):
        out = zero
        for k in range(4):
            acc = zero
            for a in range(5):
                for b in range(5):
                    acc = acc + kb[5 * a + b] * pb[b, 4 * g + k + a]
            out = jnp.where(lanes >> 5 == k, roll(acc, 32 * k), out)
        part[g] = out
        return carry

    lax.fori_loop(0, GROUPS, group, 0)


def outer_conv(tiles, wide, narrow, kb, part, rows_ref, cols_ref, hid):
    lanes = iota((CH, LANES), 1)
    zero = jnp.zeros((CH, LANES), F32)
    above = dot(tiles[0], wide[0]) + dot(tiles[1], wide[1]) + dot(tiles[2], wide[2])
    below = dot(tiles[5], wide[3]) + dot(tiles[6], wide[4]) + dot(tiles[7], wide[5])
    left, right = dot(tiles[3], narrow[0]), dot(tiles[4], narrow[1])
    rows = (above[:, :LANES], above[:, LANES:], below[:, :LANES], below[:, LANES:])
    for i in range(4):
        rows_ref[i] = rows[i]
    cols_ref[0], cols_ref[1] = left, right
    first, second, last, prior = zero, zero, zero, zero
    for b in range(5):
        r0, r1, r2, r3 = [roll(row, -b) if b else row for row in rows]
        first = first + kb[b] * r0 + kb[5 + b] * r1
        second = second + kb[b] * r1
        prior = prior + kb[20 + b] * r2
        last = last + kb[15 + b] * r2 + kb[20 + b] * r3
    even = lanes & 1 == 0
    low, high = zero, zero
    for a in range(5):
        one = roll(left, -2 * (a - 2))
        low = low + kb[5 * a] * one + jnp.where(even, kb[5 * a + 1] * roll(one, -1), 0.0)
        one = roll(right, -2 * (a - 2))
        high = high + kb[5 * a + 4] * one + jnp.where(even, 0.0, kb[5 * a + 3] * roll(one, 1))
    for g in range(GROUPS):
        extra = zero
        for k in range(4):
            u = 4 * g + k
            extra = jnp.where(lanes >> 1 == 16 * k, roll(low, 32 * k - 2 * u), extra)
            extra = jnp.where(lanes >> 1 == 16 * k + 15, roll(high, 32 * k + 30 - 2 * u), extra)
        total = part[g] + extra
        if g == 0:
            total = total + jnp.where(lanes < 32, first, jnp.where(lanes < 64, roll(second, 32), 0.0))
        if g == GROUPS - 1:
            total = total + jnp.where(lanes >= 96, roll(last, 96), jnp.where(lanes >= 64, roll(prior, 64), 0.0))
        hid[g] = total.astype(BF16)


def complete_rows(rows_ref, cols_ref, pb):
    lanes = iota((CH, LANES), 1)
    left, right = cols_ref[0], cols_ref[1]
    for i, r in enumerate((0, 1, 34, 35)):
        for b in range(5):
            pb[b, r] = roll(rows_ref[i], -b) if b else rows_ref[i]
    for r in range(SIDE):
        row = jnp.where(lanes < 2, roll(left, -2 * r), pb[0, r + 2])
        row = jnp.where(lanes >> 1 == 17, roll(right, 34 - 2 * r), row)
        for b in range(5):
            pb[b, r + 2] = roll(row, -b) if b else row


def outer_spread(gh, kb, border):
    lanes = iota((CH, LANES), 1)
    zero = jnp.zeros((CH, LANES), F32)
    own = lanes < 32
    first, last = gh[0].astype(F32), gh[GROUPS - 1].astype(F32)
    r0, r1 = jnp.where(own, first, 0.0), jnp.where(own, roll(first, -32), 0.0)
    r30, r31 = jnp.where(own, roll(last, -64), 0.0), jnp.where(own, roll(last, -96), 0.0)
    gp = [zero] * 4
    for b in range(5):
        s0, s1, s30, s31 = [roll(row, b) if b else row for row in (r0, r1, r30, r31)]
        gp[0] = gp[0] + kb[b] * s0
        gp[1] = gp[1] + kb[b] * s1 + kb[5 + b] * s0
        gp[2] = gp[2] + kb[15 + b] * s31 + kb[20 + b] * s30
        gp[3] = gp[3] + kb[20 + b] * s31
    head, tail = zero, zero
    for g in range(GROUPS):
        chunk = gh[g].astype(F32)
        for k in range(4):
            r = 4 * g + k
            head = jnp.where(lanes >> 1 == r, roll(chunk, 2 * r - 32 * k), head)
            tail = jnp.where(lanes >> 1 == r, roll(chunk, 2 * r - 32 * k - 30), tail)
    even = lanes & 1 == 0
    left, right = zero, zero
    for a in range(5):
        one = roll(head, 2 * (a - 2))
        left = left + kb[5 * a] * one + jnp.where(even, 0.0, kb[5 * a + 1] * roll(one, 1))
        one = roll(tail, 2 * (a - 2))
        right = right + kb[5 * a + 4] * one + jnp.where(even, kb[5 * a + 3] * roll(one, -1), 0.0)
    top, bottom, corners = zero, zero, zero
    for line in range(2):
        upper, lower = gp[line], gp[2 + line]
        top = jnp.where(lanes >> 5 == line, roll(upper, 32 * line - 2), top)
        bottom = jnp.where(lanes >> 5 == line, roll(lower, 32 * line - 2), bottom)
        for i, (row, start) in enumerate(((upper, 0), (upper, 34), (lower, 0), (lower, 34))):
            corners = jnp.where(lanes >> 1 == 2 * i + line, roll(row, 4 * i + 2 * line - start), corners)
    for i, wide in enumerate((top, left, right, bottom, corners)):
        border[i] = fold(wide).astype(BF16)


def inner_spread(gh, go_ref, kb, gb, acc_ref):
    lanes = iota((CH, LANES), 1)
    zero = jnp.zeros((CH, LANES), F32)
    for r in (0, 1, 34, 35):
        for b in range(5):
            gb[b, r] = zero
    for g in range(GROUPS):
        chunk = gh[g].astype(F32)
        for k in range(4):
            row = jnp.where(lanes < 32, roll(chunk, -32 * k) if k else chunk, 0.0)
            for b in range(5):
                gb[b, 4 * g + k + 2] = row if b == 2 else roll(row, b - 2)
        acc_ref[g] = go_ref[:, LANES * g : LANES * (g + 1)].astype(F32)

    def group(g, carry):
        out = zero
        for k in range(4):
            acc = zero
            for a in range(5):
                for b in range(5):
                    acc = acc + kb[5 * a + b] * gb[b, 4 * g + (k + 4 - a)]
            out = jnp.where(lanes >> 5 == k, roll(acc, 32 * k), out)
        acc_ref[g] = acc_ref[g] + out
        return carry

    lax.fori_loop(0, GROUPS, group, 0)


def tap_sums(pb, gb, ka):
    zero = jnp.zeros((CH, LANES), F32)
    for b in range(5):

        def taps(u, sums, b=b):
            grad = gb[2, u + 2]
            return tuple(sums[a] + grad * pb[b, u + a] for a in range(5))

        sums = lax.fori_loop(0, SIDE, taps, (zero,) * 5)
        for a in range(5):
            ka[5 * a + b] = sums[a]
    for tap in range(TAPS, 28):
        ka[tap] = zero
    totals = dot(jnp.ones((8, LANES), F32), ka[...].reshape(28 * CH, LANES), ((1,), (1,)), lax.Precision.HIGHEST)
    sub = iota((8, LANES), 0)
    out = jnp.zeros((8, LANES), F32)
    for i in range(7):
        out = jnp.where(sub == i, totals[:, LANES * i : LANES * (i + 1)], out)
    return out


class Place:
    def __init__(self):
        self.tile, self.chan = lax.axis_index("tile"), lax.axis_index("chan")
        self.z = lax.rem(self.tile, NZ)
        self.xy = lax.div(self.tile, NZ)
        self.x = lax.rem(self.xy, NX)
        self.yl = lax.div(self.xy, NX)
        self.core = lax.rem(self.chan, 2)
        self.yh = lax.div(self.chan, 2)
        self.y = self.yh * NYL + self.yl

    def at(self, tile, chan):
        return {"tile": tile, "chan": chan}

    def along_z(self, k):
        return self.at(self.xy * NZ + lax.rem(self.z + k, NZ), self.chan)

    def tile_xy(self, k):
        return lax.rem(self.xy + k, NXY) * NZ + self.z

    def along_xy(self, k):
        return self.at(self.tile_xy(k), self.chan)

    def along_x(self, k):
        return self.at((self.yl * NX + lax.rem(self.x + k, NX)) * NZ + self.z, self.chan)

    def along_yl(self, k):
        return self.at((lax.rem(self.yl + k, NYL) * NX + self.x) * NZ + self.z, self.chan)

    def along_y(self, k):
        y = lax.rem(self.y + k, NY)
        return self.at((lax.rem(y, NYL) * NX + self.x) * NZ + self.z, lax.div(y, NYL) * 2 + self.core)

    def along_chan(self, k):
        return self.at(self.tile, lax.rem(self.chan + k, NCHAN))

    def partner(self):
        return self.at(self.tile, self.yh * 2 + (1 - self.core))


def send(src, dst, sems, k, device):
    copy = pltpu.make_async_remote_copy(
        src_ref=src, dst_ref=dst, send_sem=sems[0].at[k], recv_sem=sems[1].at[k], device_id=device, device_id_type=MESH
    )
    copy.start()
    return copy


def landed(copies):
    for copy in copies:
        copy.wait_recv()


def z_slot(z, tile):
    behind = lax.rem(z - lax.rem(tile, NZ) + NZ, NZ)
    m = behind & 3
    return m * 3 + lax.rem((behind >> 2) + ((m + 1) >> 2), 3)


Z_STEPS = (0, 1, 2, 11)
BLOCK = 32
NEAR = (1, 7, 2, 6, 3, 5, 4)
FAR = (4, 3, 5, 2, 6, 1, 7, 0)


def scratch_shapes():
    rows, tile = (CH, LANES), (16, LANES)
    vmem = dict(
        x=((CH, 1024), BF16), go=((CH, 1024), BF16), taps=((TAPS, CH), BF16), win=((FULL, HID), BF16), wout=((HID, FULL), BF16),
        rim=((4, *tile), BF16), zbuf=((NZ, 4, *tile), BF16), xout=((NXY, 5, *tile), BF16), xgot=((NXY, 5, *tile), BF16),
        wide=((6, LANES, 2 * LANES), BF16), narrow=((2, LANES, LANES), BF16), places=((3, LANES, 1024), BF16),
        kb=((TAPS, *rows), F32), pb=((5, PADS, *rows), F32), gb=((5, PADS, *rows), F32), ka=((28, *rows), F32),
        part=((GROUPS, *rows), F32), rows=((4, *rows), F32), cols=((2, *rows), F32), acc=((GROUPS, *rows), F32),
        hid=((GROUPS, *rows), BF16), feat=((GROUPS, *rows), BF16), cot=((GROUPS, *rows), BF16),
        br=((GROUPS, *rows), BF16), gf=((GROUPS, *rows), BF16), bo=((GROUPS, *rows), BF16), gh=((GROUPS, *rows), BF16),
        border=((5, *tile), BF16), bz=((NZ, 5, *tile), BF16), bout=((NXY, 5, *tile), BF16), bgot=((NXY, 5, *tile), BF16),
        kown=((4, 8, LANES), F32), kz=((6, 8, LANES), F32), kxy=((NXY, 8, LANES), F32),
        grads=((2, NX, FULL, FULL), F32), terms=((2, NX, FULL, FULL), BF16), rcore=((NX, FULL, FULL), BF16),
        sx=((FULL, FULL), F32), tx=((NX, FULL, FULL), BF16), rx=((NX, NY, BLOCK, FULL), BF16),
        sy=((BLOCK, FULL), F32), ty=((NY, BLOCK, FULL), BF16), ry=((NY, BLOCK, FULL), BF16),
        tz=((BLOCK, FULL), BF16), uz=((BLOCK, FULL), BF16), rz=((7, BLOCK, FULL), BF16),
    )
    sems = dict(
        z=NZ, cot=NCHAN, xy=NXY, s1=NCHAN, s2a=NCHAN, s2b=NCHAN, core=NX, x=NX * NY, y=NY, sz=6, bz=NZ, bxy=NXY,
        kz=6, kxy=NXY, kc=NCHAN, ay=NY, ax=NX * NY, ac=NX * NY,
    )
    return vmem, sems


class Names:
    pass


def step_kernel(
    nb_hbm, rot_hbm, x_hbm, go_hbm, k_hbm, win_hbm, wout_hbm, out_ref, gin_ref, all_ref, kall_ref, load_sem, nb_ref, rot_ref, *rest
):
    vmem, semaphores = scratch_shapes()
    s, sem = Names(), Names()
    for name, ref in zip(vmem, rest):
        setattr(s, name, ref)
    rest = rest[len(vmem) :]
    for index, name in enumerate(semaphores):
        setattr(sem, name, rest[2 * index : 2 * index + 2])
    at = Place()
    copies = []

    def go(*args):
        copies.append(send(*args))
        return copies[-1]

    def first_along_z(src, slots, sems):
        slots[0] = src[...]
        far = [go(src, slots.at[j], sems, j, at.along_z(4 * j)) for j in (1, 2)]
        return far, [go(src, slots.at[3 * m], sems, 3 * m, at.along_z(Z_STEPS[m])) for m in (2, 1, 3)]

    def then_along_z(far, near, slots, sems):
        for j in (1, 2):
            landed([far[j - 1]])
            near += [go(slots.at[j], slots.at[3 * m + j], sems, 3 * m + j, at.along_z(Z_STEPS[m])) for m in (2, 1, 3)]

    barrier = pltpu.get_barrier_semaphore()
    peers = (
        [at.along_z(k) for k in (1, 2, 4, 8, 10, 11)]
        + [at.along_xy(k) for k in range(1, NXY)]
        + [at.along_chan(k) for k in range(1, NCHAN)]
        + [at.along_y(k) for k in range(1, NY)]
    )
    for device in peers:
        pl.semaphore_signal(barrier, inc=1, device_id=device, device_id_type=MESH)
    pairs = ((x_hbm, s.x), (go_hbm, s.go), (k_hbm, s.taps), (win_hbm, s.win), (wout_hbm, s.wout), (nb_hbm, nb_ref), (rot_hbm, rot_ref))
    loads = [pltpu.make_async_copy(src, dst, load_sem.at[i]) for i, (src, dst) in enumerate(pairs)]
    for load in loads:
        load.start()
    loads[0].wait()
    rims_of(s.x, s.rim)
    loads[1].wait()
    pl.semaphore_wait(barrier, len(peers))

    far, z_in = first_along_z(s.rim, s.zbuf, sem.z)
    cot_in = []
    for k in range(1, NCHAN):
        chan = lax.rem(at.chan + k, NCHAN)
        chunk = s.go.at[:, pl.ds(pl.multiple_of(chan * LANES, LANES), LANES)]
        cot_in.append(go(chunk, s.cot.at[at.chan], sem.cot, k, at.along_chan(k)))
    s.cot[at.chan] = s.go[:, pl.ds(pl.multiple_of(at.chan * LANES, LANES), LANES)]
    for load in (loads[2], loads[5], loads[6]):
        load.wait()
    spread_taps(s.taps, s.kb)
    make_picks(rot_ref, at.tile, s.wide, s.narrow)
    then_along_z(far, z_in, s.zbuf, sem.z)
    inner_conv(s.x, s.kb, s.pb, s.part)
    landed(z_in)
    lane = iota((16, LANES), 1)
    xy_in = []
    for k in (6, 2, 5, 7, 1, 3, 4, 0):
        tile = at.tile_xy(k)
        packed = jnp.zeros((16, LANES), F32)
        for i in range(4):
            d = EDGE_DIRS[i]
            s.xout[k, i] = s.zbuf[z_slot(at.z, nb_ref[d, tile]), (rot_ref[d, tile] + BASE[d]) & 3]
            d = CORNER_DIRS[i]
            edge = s.zbuf[z_slot(at.z, nb_ref[d, tile]), (rot_ref[d, tile] + BASE[d]) & 3].astype(F32)
            packed = jnp.where(((lane + 2) & 31) >> 2 == i, roll(edge, 4 * i) if i else edge, packed)
        s.xout[k, 4] = packed.astype(BF16)
        if k:
            xy_in.append(go(s.xout.at[k], s.xgot.at[k], sem.xy, k, at.along_xy(k)))
    s.xgot[0] = s.xout[0]
    make_places(nb_ref, rot_ref, at.tile, s.places)
    loads[3].wait()
    loads[4].wait()
    landed(xy_in)
    tiles = [None] * 8
    for i in range(4):
        d = EDGE_DIRS[i]
        slot = lax.rem(at.xy - lax.div(nb_ref[d, at.tile], NZ) + NXY, NXY)
        tiles[d] = unfold(s.xgot[slot, i].astype(F32))
        d = CORNER_DIRS[i]
        slot = lax.rem(at.xy - lax.div(nb_ref[d, at.tile], NZ) + NXY, NXY)
        packed = s.xgot[slot, 4].astype(F32)
        tiles[d] = unfold(roll(packed, -4 * i) if i else packed)
    outer_conv(tiles, s.wide, s.narrow, s.kb, s.part, s.rows, s.cols, s.hid)

    def swap(src, dst, sems):
        moved = []
        for k in (4, 5, 3, 6, 2, 7, 1):
            chan = lax.rem(at.chan + k, NCHAN)
            moved.append(go(src.at[chan], dst.at[at.chan], sems, k, at.along_chan(k)))
        dst[at.chan] = src[at.chan]
        return moved

    feat_in = swap(s.hid, s.feat, sem.s1)
    complete_rows(s.rows, s.cols, s.pb)
    landed(cot_in)
    landed(feat_in)

    feat = s.feat[...].reshape(FULL, LANES)
    cot = s.cot[...].reshape(FULL, LANES)
    branch = jnp.zeros((FULL, LANES), F32)
    gfeat = jnp.zeros((FULL, LANES), F32)
    core_in = []
    for part in range(NX):
        lo = FULL * part
        w_in = s.win[:, lo : lo + FULL]
        w_out = s.wout[lo : lo + FULL, :]
        pre = dot(w_in, feat, ((0,), (0,)))
        cumul = 0.5 * (1.0 + lax.erf(pre * 0.7071067811865476))
        act = (pre * cumul).astype(BF16)
        gact = dot(w_out, cot)
        slope = cumul + pre * jnp.exp(-0.5 * pre * pre) * 0.3989422804014327
        gpre = (gact * slope).astype(BF16)
        branch = branch + dot(w_out, act, ((0,), (0,)))
        gfeat = gfeat + dot(w_in, gpre)
        for side, value in enumerate((dot(act, cot, ((1,), (1,))), dot(feat, gpre, ((1,), (1,))))):
            s.grads[side, part] = value
            s.terms[side, part] = value.astype(BF16)
        core_in.append(go(s.terms.at[1 - at.core, part], s.rcore.at[part], sem.core, part, at.partner()))
    s.br[...] = branch.astype(BF16).reshape(GROUPS, CH, LANES)
    s.gf[...] = gfeat.astype(BF16).reshape(GROUPS, CH, LANES)
    grad_in = swap(s.gf, s.gh, sem.s2a)
    branch_in = swap(s.br, s.bo, sem.s2b)

    landed(core_in)
    x_in = {}
    for k in (2, 1, 3, 0):
        part = lax.rem(at.x + k, NX)
        total = s.grads[at.core, part] + s.rcore[part].astype(F32)
        if k == 0:
            s.sx[...] = total
            continue
        s.tx[k] = total.astype(BF16)
        for step in FAR:
            rows = pl.ds(pl.multiple_of(lax.rem(at.y + step, NY) * BLOCK, BLOCK), BLOCK)
            x_in[k, step] = go(s.tx.at[k, rows], s.rx.at[k, step], sem.x, k * NY + step, at.along_x(k))

    landed(grad_in)
    outer_spread(s.gh, s.kb, s.border)
    far, border_in = first_along_z(s.border, s.bz, sem.bz)
    inner_spread(s.gh, s.go, s.kb, s.gb, s.acc)
    then_along_z(far, border_in, s.bz, sem.bz)

    y_in = {}
    for step in FAR:
        landed([x_in[k, step] for k in (1, 3, 2)])
        total = s.sx[pl.ds(pl.multiple_of(lax.rem(at.y + step, NY) * BLOCK, BLOCK), BLOCK)]
        for k in range(1, NX):
            total = total + s.rx[k, step].astype(F32)
        if step == 0:
            s.sy[...] = total
            continue
        s.ty[step] = total.astype(BF16)
        y_in[step] = go(s.ty.at[step], s.ry.at[step], sem.y, step, at.along_y(step))

    s.kown[0] = tap_sums(s.pb, s.gb, s.ka)
    taps_far = [go(s.kown.at[0], s.kz.at[j], sem.kz, j, at.along_z(4 * j)) for j in (1, 2)]

    landed(branch_in)
    for g in range(GROUPS):
        span = slice(LANES * g, LANES * (g + 1))
        out_ref[:, span] = (s.x[:, span].astype(F32) + s.bo[g].astype(F32)).astype(BF16)

    landed([y_in[step] for step in NEAR])
    total = s.sy[...]
    for step in range(1, NY):
        total = total + s.ry[step].astype(F32)
    s.tz[...] = total.astype(BF16)
    s.rz[0] = s.tz[...]
    sum_far = [go(s.tz, s.rz.at[j], sem.sz, j, at.along_z(4 * j)) for j in (1, 2)]
    landed(taps_far)
    s.kown[1] = s.kown[0] + s.kz[1] + s.kz[2]
    taps_near = [go(s.kown.at[1], s.kz.at[2 + m], sem.kz, 2 + m, at.along_z(Z_STEPS[m])) for m in (2, 1, 3)]

    landed(border_in)
    border_xy = []
    for k in (6, 2, 5, 7, 1, 3, 4, 0):
        tile = at.tile_xy(k)
        packed = jnp.zeros((16, LANES), BF16)
        for i in range(4):
            s.bout[k, i] = s.bz[z_slot(at.z, nb_ref[7 - EDGE_DIRS[i], tile]), i]
            corner = s.bz[z_slot(at.z, nb_ref[7 - CORNER_DIRS[i], tile]), 4]
            packed = jnp.where((lane >> 2) & 15 == i, corner, packed)
        s.bout[k, 4] = packed
        if k:
            border_xy.append(go(s.bout.at[k], s.bgot.at[k], sem.bxy, k, at.along_xy(k)))
    s.bgot[0] = s.bout[0]

    landed(sum_far)
    total = jnp.zeros((BLOCK, FULL), F32)
    for third in range(3):
        total = total + s.rz[lax.rem(lax.div(at.z, 4) - third + 3, 3)].astype(F32)
    s.uz[...] = total.astype(BF16)
    s.rz[3] = s.uz[...]
    sum_near = [go(s.uz, s.rz.at[3 + m], sem.sz, 2 + m, at.along_z(Z_STEPS[m])) for m in (2, 1, 3)]

    landed(taps_near)
    s.kown[2] = s.kown[1] + s.kz[3] + s.kz[4] + s.kz[5]
    taps_xy = [go(s.kown.at[2], s.kxy.at[k], sem.kxy, k, at.along_xy(k)) for k in range(1, NXY)]

    landed(sum_near)
    total = jnp.zeros((BLOCK, FULL), F32)
    for quarter in range(4):
        total = total + s.rz[3 + ((at.z - quarter + 4) & 3)].astype(F32)
    all_ref[at.core, at.x, at.y] = (total * SCALE).astype(BF16)
    own = all_ref.at[at.core, at.x, at.y]
    y_all = {k: go(own, own, sem.ay, k, at.along_y(k)) for k in NEAR}
    x_all, core_all = {}, []

    def onward(step):
        block = all_ref.at[at.core, at.x, lax.rem(at.y - step + NY, NY)]
        for k in (2, 1, 3):
            x_all[k, step] = go(block, block, sem.ax, k * NY + step, at.along_x(k))
        core_all.append(go(block, block, sem.ac, step, at.partner()))

    onward(0)

    landed(border_xy)
    low = lane < 64
    received = []
    packed = jnp.zeros((16, LANES), F32)
    for i in range(4):
        slot = lax.rem(at.xy - lax.div(nb_ref[7 - EDGE_DIRS[i], at.tile], NZ) + NXY, NXY)
        received.append(s.bgot[slot, i].astype(F32))
        slot = lax.rem(at.xy - lax.div(nb_ref[7 - CORNER_DIRS[i], at.tile], NZ) + NXY, NXY)
        packed = jnp.where((lane >> 2) & 15 == i, s.bgot[slot, 4].astype(F32), packed)
    total = dot(unfold(packed), s.places[2])
    for pair in range(2):
        one, two = received[2 * pair : 2 * pair + 2]
        both = [jnp.where(low, one, roll(two, 64)), jnp.where(low, roll(one, 64), two)]
        total = total + dot(jnp.concatenate(both, axis=0).astype(BF16), s.places[pair])
    for g in range(GROUPS):
        span = slice(LANES * g, LANES * (g + 1))
        gin_ref[:, span] = (s.acc[g] + total[:, span]).astype(BF16)

    for step in NEAR[:2]:
        landed([y_all[step]])
        onward(step)
    landed(taps_xy)
    total = s.kown[2]
    for k in range(1, NXY):
        total = total + s.kxy[k]
    s.kown[3] = total * SCALE
    kall_ref[at.chan] = s.kown[3]
    taps_all = [go(s.kown.at[3], kall_ref.at[at.chan], sem.kc, k, at.along_chan(k)) for k in range(1, NCHAN)]
    for step in NEAR[2:]:
        landed([y_all[step]])
        onward(step)

    for step in (0, *NEAR):
        for k in (1, 3, 2):
            landed([x_all[k, step]])
            block = all_ref.at[at.core, lax.rem(at.x - k + NX, NX), lax.rem(at.y - step + NY, NY)]
            core_all.append(go(block, block, sem.ac, k * NY + step, at.partner()))
    landed(taps_all)
    landed(core_all)
    for copy in copies:
        copy.wait_send()


def last_kernel(out_ref, gin_ref, all_ref, kall_ref, out2_ref, gin2_ref, win_ref, wout_ref, kgrad_ref):
    out2_ref[...] = out_ref[...]
    gin2_ref[...] = gin_ref[...]
    for x in range(NX):
        for y in range(NY):
            row = FULL * x + BLOCK * y
            wout_ref[row : row + BLOCK, :] = all_ref[0, x, y].astype(F32)
            win_ref[BLOCK * y : BLOCK * (y + 1), FULL * x : FULL * (x + 1)] = all_ref[1, x, y].astype(F32)
    low = iota((8, LANES), 1) >> 5
    for j in range(4):
        for side in range(2):
            rows = jnp.zeros((8, LANES), F32)
            for k in range(4):
                rows = jnp.where(low == k, roll(kall_ref[4 * side + k], 32 * (k - j)), rows)
            for i in range(7):
                if 4 * i + j < TAPS:
                    kgrad_ref[4 * i + j : 4 * i + j + 1, LANES * side : LANES * (side + 1)] = rows[i : i + 1]


def body(inputs, grad_out, kernel, w_in, w_out, neighbours, rotations):
    vmem, semaphores = scratch_shapes()
    tables = [pltpu.SMEM((8, NXY * NZ), I32)] * 2
    scratch = [pltpu.SemaphoreType.DMA((7,)), *tables] + [pltpu.VMEM(shape, dtype) for shape, dtype in vmem.values()]
    for count in semaphores.values():
        scratch += [pltpu.SemaphoreType.DMA((count,))] * 2
    shapes = [((CH, 1024), BF16), ((CH, 1024), BF16), ((2, NX, NY, BLOCK, FULL), BF16), ((NCHAN, 8, LANES), F32)]
    arrays = (neighbours.T, rotations.T, inputs.reshape(CH, 1024), grad_out.reshape(CH, 1024), kernel, w_in, w_out)
    results = pl.pallas_call(
        step_kernel,
        out_shape=[jax.ShapeDtypeStruct(shape, dtype) for shape, dtype in shapes],
        in_specs=[pl.BlockSpec(memory_space=pltpu.HBM)] * 7,
        out_specs=[VMEM] * 4,
        scratch_shapes=scratch,
        compiler_params=pltpu.CompilerParams(vmem_limit_bytes=50 << 20, collective_id=1, has_side_effects=True),
        name="step",
    )(*[pltpu.with_memory_space_constraint(array, pltpu.HBM) for array in arrays])
    shapes = [((CH, 1024), BF16), ((CH, 1024), BF16), ((FULL, HID), F32), ((HID, FULL), F32), ((TAPS, FULL), F32)]
    outputs, grad_in, grad_w_in, grad_w_out, grad_kernel = pl.pallas_call(
        last_kernel,
        out_shape=[jax.ShapeDtypeStruct(shape, dtype) for shape, dtype in shapes],
        in_specs=[VMEM] * 4,
        out_specs=[VMEM] * 5,
        compiler_params=pltpu.CompilerParams(vmem_limit_bytes=12 << 20),
        name="last",
    )(*results)
    return outputs.reshape(1, CH, 1024), grad_in.reshape(1, CH, 1024), grad_w_in, grad_w_out, grad_kernel


def solution(mesh):
    split = P("tile", "chan", None)
    return jax.shard_map(
        body,
        mesh=mesh,
        in_specs=(split, split, P(None, "chan"), P(), P(), P(), P()),
        out_specs=(split, split, P(), P(), P()),
        check_vma=False,
    )
```

```python
import jax
import jax.numpy as jnp
from jax import lax
from jax.experimental import pallas as pl
from jax.experimental.pallas import tpu as pltpu
from jax.sharding import PartitionSpec as P

NX, NZ, NYL, NYH = 4, 12, 2, 4
NXY = NX * NYL
NY = NYL * NYH
NCHAN = NYH * 2
CH = 32
SIDE = 32
LANES = 128
GROUPS = 8
PADS = SIDE + 4
TAPS = 25
HID = 1024
FULL = 256
SCALE = (NXY * NZ * SIDE * SIDE) ** -0.5
MESH = pl.DeviceIdType.MESH
F32, BF16, I32 = jnp.float32, jnp.bfloat16, jnp.int32

BASE = (0, 0, 0, 3, 1, 2, 2, 2)
EDGE_DIRS = (1, 3, 4, 6)
CORNER_DIRS = (0, 2, 5, 7)

VMEM = pl.BlockSpec(memory_space=pltpu.VMEM)
SMEM = pl.BlockSpec(memory_space=pltpu.SMEM)


def iota(shape, axis):
    return lax.broadcasted_iota(I32, shape, axis)


def roll(values, shift):
    return pltpu.roll(values, shift % LANES, 1)


def dot(a, b, contract=((1,), (0,)), precision=None):
    return lax.dot_general(a, b, (contract, ((), ())), preferred_element_type=F32, precision=precision)


def turned(q, i, j):
    q0, q1, q2, q3 = [(q == k).astype(I32) for k in range(4)]
    rows = q0 * i + q1 * j + q2 * (31 - i) + q3 * (31 - j)
    cols = q0 * j + q1 * (31 - i) + q2 * (31 - j) + q3 * i
    return rows, cols


def fold(wide):
    low = iota((16, LANES), 1) < 64
    return jnp.where(low, wide[:16], roll(wide[16:], 64))


def unfold(tile):
    return jnp.concatenate([tile, roll(tile, 64)], axis=0).astype(BF16)


def spread_taps(k_ref, kb):
    taps = k_ref[...].astype(F32)
    eye = iota((CH, CH), 0) == iota((CH, CH), 1)
    ones = jnp.ones((CH, LANES), BF16)
    for tap in range(TAPS):
        row = jnp.broadcast_to(taps[tap : tap + 1, :], (CH, CH))
        kb[tap] = dot(jnp.where(eye, row, 0.0).astype(BF16), ones)


def rims_of(x_ref, rim):
    p = iota((1024, 256), 0)
    n = iota((1, 256), 1)
    e, line, i = n >> 6, (n >> 5) & 1, n & 31
    px = jnp.where(e == 0, (30 + line) * 32 + i, 0)
    px = jnp.where(e == 1, i * 32 + line, px)
    px = jnp.where(e == 2, line * 32 + i, px)
    px = jnp.where(e == 3, i * 32 + 30 + line, px)
    rims = dot(x_ref[...], jnp.where(p == px, 1.0, 0.0).astype(BF16))
    low = iota((16, LANES), 1) < 64
    for pair in range(2):
        half = rims[:, LANES * pair : LANES * (pair + 1)]
        upper, lower = half[:16], half[16:]
        rim[2 * pair] = jnp.where(low, upper, roll(lower, 64)).astype(BF16)
        rim[2 * pair + 1] = jnp.where(low, roll(upper, 64), lower).astype(BF16)


def make_picks(rot_ref, me, wide, narrow):
    def pick(d, i, j, valid):
        q = rot_ref[d, me]
        si, sj = turned(q, i, j)
        e = (q + BASE[d]) & 3
        along = (e & 1) * si + (1 - (e & 1)) * sj
        line = (1 - (e & 1)) * (si - 30 * (e == 0).astype(I32)) + (e & 1) * (sj - 30 * (e == 3).astype(I32))
        lane = jnp.where(valid, line * 32 + along, -1)
        return jnp.where(iota((LANES, lane.shape[1]), 0) == lane, 1.0, 0.0).astype(BF16)

    n = iota((1, 2 * LANES), 1)
    a, lane = n >> 7, n & 127
    for side, (first, dirs) in enumerate(((30, (0, 1, 2)), (0, (5, 6, 7)))):
        i = first + a
        wide[3 * side] = pick(dirs[0], i, 30 + lane, lane < 2)
        wide[3 * side + 1] = pick(dirs[1], i, lane - 2, (lane >= 2) & (lane < 34))
        wide[3 * side + 2] = pick(dirs[2], i, lane - 34, (lane >= 34) & (lane < 36))
    m = iota((1, LANES), 1)
    narrow[0] = pick(3, m >> 1, 30 + (m & 1), m < 64)
    narrow[1] = pick(4, m >> 1, m & 1, m < 64)


def make_places(nb_ref, rot_ref, me, places):
    k = iota((LANES, 1), 0)
    p = iota((1, 1024), 1)
    m = k & 63
    pixels = []
    for d in EDGE_DIRS:
        q = rot_ref[d, nb_ref[7 - d, me]]
        line, along = ((m >> 5), (m & 31)) if d in (1, 6) else ((m & 1), (m >> 1))
        edge = line + (30 if d in (1, 3) else 0)
        si, sj = turned(q, edge, along) if d in (1, 6) else turned(q, along, edge)
        pixels.append(si * 32 + sj)
    for pair in range(2):
        places[pair] = jnp.where(p == jnp.where(k < 64, pixels[2 * pair], pixels[2 * pair + 1]), 1.0, 0.0).astype(BF16)
    q = jnp.zeros((LANES, 1), I32)
    for index, d in enumerate(CORNER_DIRS):
        q = jnp.where(k >> 2 == index, rot_ref[d, nb_ref[7 - d, me]], q)
    i = ((k >> 1) & 1) + jnp.where(k < 8, 30, 0)
    j = (k & 1) + jnp.where((k >> 2) & 1 == 0, 30, 0)
    si, sj = turned(q, i, j)
    places[2] = jnp.where((p == si * 32 + sj) & (k < 16), 1.0, 0.0).astype(BF16)


def inner_conv(x_ref, kb, pb, part):
    lanes = iota((CH, LANES), 1)
    zero = jnp.zeros((CH, LANES), F32)
    for r in (0, 1, 34, 35):
        for b in range(5):
            pb[b, r] = zero
    for g in range(GROUPS):
        chunk = x_ref[:, LANES * g : LANES * (g + 1)].astype(F32)
        for k in range(4):
            row = jnp.where((lanes >= 2) & (lanes < 34), roll(chunk, 2 - 32 * k), 0.0)
            for b in range(5):
                pb[b, 4 * g + k + 2] = roll(row, -b) if b else row

    def group(g, carry):
        out = zero
        for k in range(4):
            acc = zero
            for a in range(5):
                for b in range(5):
                    acc = acc + kb[5 * a + b] * pb[b, 4 * g + k + a]
            out = jnp.where(lanes >> 5 == k, roll(acc, 32 * k), out)
        part[g] = out
        return carry

    lax.fori_loop(0, GROUPS, group, 0)


def outer_conv(tiles, wide, narrow, kb, part, rows_ref, cols_ref, hid):
    lanes = iota((CH, LANES), 1)
    zero = jnp.zeros((CH, LANES), F32)
    above = dot(tiles[0], wide[0]) + dot(tiles[1], wide[1]) + dot(tiles[2], wide[2])
    below = dot(tiles[5], wide[3]) + dot(tiles[6], wide[4]) + dot(tiles[7], wide[5])
    left, right = dot(tiles[3], narrow[0]), dot(tiles[4], narrow[1])
    rows = (above[:, :LANES], above[:, LANES:], below[:, :LANES], below[:, LANES:])
    for i in range(4):
        rows_ref[i] = rows[i]
    cols_ref[0], cols_ref[1] = left, right
    first, second, last, prior = zero, zero, zero, zero
    for b in range(5):
        r0, r1, r2, r3 = [roll(row, -b) if b else row for row in rows]
        first = first + kb[b] * r0 + kb[5 + b] * r1
        second = second + kb[b] * r1
        prior = prior + kb[20 + b] * r2
        last = last + kb[15 + b] * r2 + kb[20 + b] * r3
    even = lanes & 1 == 0
    low, high = zero, zero
    for a in range(5):
        one = roll(left, -2 * (a - 2))
        low = low + kb[5 * a] * one + jnp.where(even, kb[5 * a + 1] * roll(one, -1), 0.0)
        one = roll(right, -2 * (a - 2))
        high = high + kb[5 * a + 4] * one + jnp.where(even, 0.0, kb[5 * a + 3] * roll(one, 1))
    for g in range(GROUPS):
        extra = zero
        for k in range(4):
            u = 4 * g + k
            extra = jnp.where(lanes >> 1 == 16 * k, roll(low, 32 * k - 2 * u), extra)
            extra = jnp.where(lanes >> 1 == 16 * k + 15, roll(high, 32 * k + 30 - 2 * u), extra)
        total = part[g] + extra
        if g == 0:
            total = total + jnp.where(lanes < 32, first, jnp.where(lanes < 64, roll(second, 32), 0.0))
        if g == GROUPS - 1:
            total = total + jnp.where(lanes >= 96, roll(last, 96), jnp.where(lanes >= 64, roll(prior, 64), 0.0))
        hid[g] = total.astype(BF16)


def complete_rows(rows_ref, cols_ref, pb):
    lanes = iota((CH, LANES), 1)
    left, right = cols_ref[0], cols_ref[1]
    for i, r in enumerate((0, 1, 34, 35)):
        for b in range(5):
            pb[b, r] = roll(rows_ref[i], -b) if b else rows_ref[i]
    for r in range(SIDE):
        row = jnp.where(lanes < 2, roll(left, -2 * r), pb[0, r + 2])
        row = jnp.where(lanes >> 1 == 17, roll(right, 34 - 2 * r), row)
        for b in range(5):
            pb[b, r + 2] = roll(row, -b) if b else row


def outer_spread(gh, kb, border):
    lanes = iota((CH, LANES), 1)
    zero = jnp.zeros((CH, LANES), F32)
    own = lanes < 32
    first, last = gh[0].astype(F32), gh[GROUPS - 1].astype(F32)
    r0, r1 = jnp.where(own, first, 0.0), jnp.where(own, roll(first, -32), 0.0)
    r30, r31 = jnp.where(own, roll(last, -64), 0.0), jnp.where(own, roll(last, -96), 0.0)
    gp = [zero] * 4
    for b in range(5):
        s0, s1, s30, s31 = [roll(row, b) if b else row for row in (r0, r1, r30, r31)]
        gp[0] = gp[0] + kb[b] * s0
        gp[1] = gp[1] + kb[b] * s1 + kb[5 + b] * s0
        gp[2] = gp[2] + kb[15 + b] * s31 + kb[20 + b] * s30
        gp[3] = gp[3] + kb[20 + b] * s31
    head, tail = zero, zero
    for g in range(GROUPS):
        chunk = gh[g].astype(F32)
        for k in range(4):
            r = 4 * g + k
            head = jnp.where(lanes >> 1 == r, roll(chunk, 2 * r - 32 * k), head)
            tail = jnp.where(lanes >> 1 == r, roll(chunk, 2 * r - 32 * k - 30), tail)
    even = lanes & 1 == 0
    left, right = zero, zero
    for a in range(5):
        one = roll(head, 2 * (a - 2))
        left = left + kb[5 * a] * one + jnp.where(even, 0.0, kb[5 * a + 1] * roll(one, 1))
        one = roll(tail, 2 * (a - 2))
        right = right + kb[5 * a + 4] * one + jnp.where(even, kb[5 * a + 3] * roll(one, -1), 0.0)
    top, bottom, corners = zero, zero, zero
    for line in range(2):
        upper, lower = gp[line], gp[2 + line]
        top = jnp.where(lanes >> 5 == line, roll(upper, 32 * line - 2), top)
        bottom = jnp.where(lanes >> 5 == line, roll(lower, 32 * line - 2), bottom)
        for i, (row, start) in enumerate(((upper, 0), (upper, 34), (lower, 0), (lower, 34))):
            corners = jnp.where(lanes >> 1 == 2 * i + line, roll(row, 4 * i + 2 * line - start), corners)
    for i, wide in enumerate((top, left, right, bottom, corners)):
        border[i] = fold(wide).astype(BF16)


def inner_spread(gh, go_ref, kb, gb, acc_ref):
    lanes = iota((CH, LANES), 1)
    zero = jnp.zeros((CH, LANES), F32)
    for r in (0, 1, 34, 35):
        for b in range(5):
            gb[b, r] = zero
    for g in range(GROUPS):
        chunk = gh[g].astype(F32)
        for k in range(4):
            row = jnp.where(lanes < 32, roll(chunk, -32 * k) if k else chunk, 0.0)
            for b in range(5):
                gb[b, 4 * g + k + 2] = row if b == 2 else roll(row, b - 2)
        acc_ref[g] = go_ref[:, LANES * g : LANES * (g + 1)].astype(F32)

    def group(g, carry):
        out = zero
        for k in range(4):
            acc = zero
            for a in range(5):
                for b in range(5):
                    acc = acc + kb[5 * a + b] * gb[b, 4 * g + (k + 4 - a)]
            out = jnp.where(lanes >> 5 == k, roll(acc, 32 * k), out)
        acc_ref[g] = acc_ref[g] + out
        return carry

    lax.fori_loop(0, GROUPS, group, 0)


def tap_sums(pb, gb, ka):
    zero = jnp.zeros((CH, LANES), F32)
    for b in range(5):

        def taps(u, sums, b=b):
            grad = gb[2, u + 2]
            return tuple(sums[a] + grad * pb[b, u + a] for a in range(5))

        sums = lax.fori_loop(0, SIDE, taps, (zero,) * 5)
        for a in range(5):
            ka[5 * a + b] = sums[a]
    for tap in range(TAPS, 28):
        ka[tap] = zero
    totals = dot(jnp.ones((8, LANES), F32), ka[...].reshape(28 * CH, LANES), ((1,), (1,)), lax.Precision.HIGHEST)
    sub = iota((8, LANES), 0)
    out = jnp.zeros((8, LANES), F32)
    for i in range(7):
        out = jnp.where(sub == i, totals[:, LANES * i : LANES * (i + 1)], out)
    return out


class Place:
    def __init__(self):
        self.tile, self.chan = lax.axis_index("tile"), lax.axis_index("chan")
        self.z = lax.rem(self.tile, NZ)
        self.xy = lax.div(self.tile, NZ)
        self.x = lax.rem(self.xy, NX)
        self.yl = lax.div(self.xy, NX)
        self.core = lax.rem(self.chan, 2)
        self.yh = lax.div(self.chan, 2)
        self.y = self.yh * NYL + self.yl

    def at(self, tile, chan):
        return {"tile": tile, "chan": chan}

    def along_z(self, k):
        return self.at(self.xy * NZ + lax.rem(self.z + k, NZ), self.chan)

    def tile_xy(self, k):
        return lax.rem(self.xy + k, NXY) * NZ + self.z

    def along_xy(self, k):
        return self.at(self.tile_xy(k), self.chan)

    def along_x(self, k):
        return self.at((self.yl * NX + lax.rem(self.x + k, NX)) * NZ + self.z, self.chan)

    def along_yl(self, k):
        return self.at((lax.rem(self.yl + k, NYL) * NX + self.x) * NZ + self.z, self.chan)

    def along_y(self, k):
        y = lax.rem(self.y + k, NY)
        return self.at((lax.rem(y, NYL) * NX + self.x) * NZ + self.z, lax.div(y, NYL) * 2 + self.core)

    def along_chan(self, k):
        return self.at(self.tile, lax.rem(self.chan + k, NCHAN))

    def partner(self):
        return self.at(self.tile, self.yh * 2 + (1 - self.core))


def send(src, dst, sems, k, device):
    copy = pltpu.make_async_remote_copy(
        src_ref=src, dst_ref=dst, send_sem=sems[0].at[k], recv_sem=sems[1].at[k], device_id=device, device_id_type=MESH
    )
    copy.start()
    return copy


def landed(copies):
    for copy in copies:
        copy.wait_recv()


def z_slot(z, tile):
    behind = lax.rem(z - lax.rem(tile, NZ) + NZ, NZ)
    m = behind & 3
    return m * 3 + lax.rem((behind >> 2) + ((m + 1) >> 2), 3)


Z_STEPS = (0, 1, 2, 11)
BLOCK = 32
NEAR = (1, 7, 2, 6, 3, 5, 4)
PAIRS = (2, 1, 3, 0)


def scratch_shapes():
    rows, tile = (CH, LANES), (16, LANES)
    vmem = dict(
        x=((CH, 1024), BF16), go=((CH, 1024), BF16), taps=((TAPS, CH), BF16), win=((FULL, HID), BF16), wout=((HID, FULL), BF16),
        rim=((4, *tile), BF16), zbuf=((NZ, 4, *tile), BF16), xout=((NXY, 5, *tile), BF16), xgot=((NXY, 5, *tile), BF16),
        wide=((6, LANES, 2 * LANES), BF16), narrow=((2, LANES, LANES), BF16), places=((3, LANES, 1024), BF16),
        kb=((TAPS, *rows), F32), pb=((5, PADS, *rows), F32), gb=((5, PADS, *rows), F32), ka=((28, *rows), F32),
        part=((GROUPS, *rows), F32), rows=((4, *rows), F32), cols=((2, *rows), F32), acc=((GROUPS, *rows), F32),
        hid=((GROUPS, *rows), BF16), feat=((GROUPS, *rows), BF16), cot=((GROUPS, *rows), BF16),
        br=((GROUPS, *rows), BF16), gf=((GROUPS, *rows), BF16), bo=((GROUPS, *rows), BF16), gh=((GROUPS, *rows), BF16),
        border=((5, *tile), BF16), bz=((NZ, 5, *tile), BF16), bout=((NXY, 5, *tile), BF16), bgot=((NXY, 5, *tile), BF16),
        kown=((4, 8, LANES), F32), kz=((6, 8, LANES), F32), kxy=((NXY, 8, LANES), F32),
        grads=((2, NX, FULL, FULL), F32), terms=((2, NX, FULL, FULL), BF16), rcore=((NX, FULL, FULL), BF16),
        sx=((FULL, FULL), F32), tx=((NX, FULL, FULL), BF16), rx=((NX, 4, 2 * BLOCK, FULL), BF16),
        sp=((2 * BLOCK, FULL), F32), ty=((4, 2 * BLOCK, FULL), BF16), ry=((NY, BLOCK, FULL), BF16),
        tz=((BLOCK, FULL), BF16), uz=((BLOCK, FULL), BF16), rz=((7, BLOCK, FULL), BF16),
    )
    sems = dict(
        z=NZ, cot=NCHAN, xy=NXY, s1=NCHAN, s2a=NCHAN, s2b=NCHAN, core=NX, x=NX * 4, y=NY, sz=6, bz=NZ, bxy=NXY,
        kz=6, kxy=NXY, kc=NCHAN, ay=NY, ax=NX * NY, ac=NX,
    )
    return vmem, sems


class Names:
    pass


def step_kernel(
    nb_hbm, rot_hbm, x_hbm, go_hbm, k_hbm, win_hbm, wout_hbm, out_ref, gin_ref, all_ref, kall_ref, load_sem, nb_ref, rot_ref, *rest
):
    vmem, semaphores = scratch_shapes()
    s, sem = Names(), Names()
    for name, ref in zip(vmem, rest):
        setattr(s, name, ref)
    rest = rest[len(vmem) :]
    for index, name in enumerate(semaphores):
        setattr(sem, name, rest[2 * index : 2 * index + 2])
    at = Place()
    copies = []

    def go(*args):
        copies.append(send(*args))
        return copies[-1]

    def first_along_z(src, slots, sems):
        slots[0] = src[...]
        far = [go(src, slots.at[j], sems, j, at.along_z(4 * j)) for j in (1, 2)]
        return far, [go(src, slots.at[3 * m], sems, 3 * m, at.along_z(Z_STEPS[m])) for m in (2, 1, 3)]

    def then_along_z(far, near, slots, sems):
        for j in (1, 2):
            landed([far[j - 1]])
            near += [go(slots.at[j], slots.at[3 * m + j], sems, 3 * m + j, at.along_z(Z_STEPS[m])) for m in (2, 1, 3)]

    barrier = pltpu.get_barrier_semaphore()
    peers = (
        [at.along_z(k) for k in (1, 2, 4, 8, 10, 11)]
        + [at.along_xy(k) for k in range(1, NXY)]
        + [at.along_chan(k) for k in range(1, NCHAN)]
        + [at.along_y(k) for k in range(1, NY)]
    )
    for device in peers:
        pl.semaphore_signal(barrier, inc=1, device_id=device, device_id_type=MESH)
    pairs = ((x_hbm, s.x), (go_hbm, s.go), (k_hbm, s.taps), (win_hbm, s.win), (wout_hbm, s.wout), (nb_hbm, nb_ref), (rot_hbm, rot_ref))
    loads = [pltpu.make_async_copy(src, dst, load_sem.at[i]) for i, (src, dst) in enumerate(pairs)]
    for load in loads:
        load.start()
    loads[0].wait()
    rims_of(s.x, s.rim)
    loads[1].wait()
    pl.semaphore_wait(barrier, len(peers))

    far, z_in = first_along_z(s.rim, s.zbuf, sem.z)
    cot_in = []
    for k in range(1, NCHAN):
        chan = lax.rem(at.chan + k, NCHAN)
        chunk = s.go.at[:, pl.ds(pl.multiple_of(chan * LANES, LANES), LANES)]
        cot_in.append(go(chunk, s.cot.at[at.chan], sem.cot, k, at.along_chan(k)))
    s.cot[at.chan] = s.go[:, pl.ds(pl.multiple_of(at.chan * LANES, LANES), LANES)]
    for load in (loads[2], loads[5], loads[6]):
        load.wait()
    spread_taps(s.taps, s.kb)
    make_picks(rot_ref, at.tile, s.wide, s.narrow)
    then_along_z(far, z_in, s.zbuf, sem.z)
    inner_conv(s.x, s.kb, s.pb, s.part)
    landed(z_in)
    lane = iota((16, LANES), 1)
    xy_in = []
    for k in (6, 2, 5, 7, 1, 3, 4, 0):
        tile = at.tile_xy(k)
        packed = jnp.zeros((16, LANES), F32)
        for i in range(4):
            d = EDGE_DIRS[i]
            s.xout[k, i] = s.zbuf[z_slot(at.z, nb_ref[d, tile]), (rot_ref[d, tile] + BASE[d]) & 3]
            d = CORNER_DIRS[i]
            edge = s.zbuf[z_slot(at.z, nb_ref[d, tile]), (rot_ref[d, tile] + BASE[d]) & 3].astype(F32)
            packed = jnp.where(((lane + 2) & 31) >> 2 == i, roll(edge, 4 * i) if i else edge, packed)
        s.xout[k, 4] = packed.astype(BF16)
        if k:
            xy_in.append(go(s.xout.at[k], s.xgot.at[k], sem.xy, k, at.along_xy(k)))
    s.xgot[0] = s.xout[0]
    make_places(nb_ref, rot_ref, at.tile, s.places)
    loads[3].wait()
    loads[4].wait()
    landed(xy_in)
    tiles = [None] * 8
    for i in range(4):
        d = EDGE_DIRS[i]
        slot = lax.rem(at.xy - lax.div(nb_ref[d, at.tile], NZ) + NXY, NXY)
        tiles[d] = unfold(s.xgot[slot, i].astype(F32))
        d = CORNER_DIRS[i]
        slot = lax.rem(at.xy - lax.div(nb_ref[d, at.tile], NZ) + NXY, NXY)
        packed = s.xgot[slot, 4].astype(F32)
        tiles[d] = unfold(roll(packed, -4 * i) if i else packed)
    outer_conv(tiles, s.wide, s.narrow, s.kb, s.part, s.rows, s.cols, s.hid)

    def swap(src, dst, sems):
        moved = []
        for k in (4, 5, 3, 6, 2, 7, 1):
            chan = lax.rem(at.chan + k, NCHAN)
            moved.append(go(src.at[chan], dst.at[at.chan], sems, k, at.along_chan(k)))
        dst[at.chan] = src[at.chan]
        return moved

    feat_in = swap(s.hid, s.feat, sem.s1)
    complete_rows(s.rows, s.cols, s.pb)
    landed(cot_in)
    landed(feat_in)

    feat = s.feat[...].reshape(FULL, LANES)
    cot = s.cot[...].reshape(FULL, LANES)
    branch = jnp.zeros((FULL, LANES), F32)
    gfeat = jnp.zeros((FULL, LANES), F32)
    core_in = []
    for part in range(NX):
        lo = FULL * part
        w_in = s.win[:, lo : lo + FULL]
        w_out = s.wout[lo : lo + FULL, :]
        pre = dot(w_in, feat, ((0,), (0,)))
        cumul = 0.5 * (1.0 + lax.erf(pre * 0.7071067811865476))
        act = (pre * cumul).astype(BF16)
        gact = dot(w_out, cot)
        slope = cumul + pre * jnp.exp(-0.5 * pre * pre) * 0.3989422804014327
        gpre = (gact * slope).astype(BF16)
        branch = branch + dot(w_out, act, ((0,), (0,)))
        gfeat = gfeat + dot(w_in, gpre)
        for side, value in enumerate((dot(act, cot, ((1,), (1,))), dot(feat, gpre, ((1,), (1,))))):
            s.grads[side, part] = value
            s.terms[side, part] = value.astype(BF16)
        core_in.append(go(s.terms.at[1 - at.core, part], s.rcore.at[part], sem.core, part, at.partner()))
    s.br[...] = branch.astype(BF16).reshape(GROUPS, CH, LANES)
    s.gf[...] = gfeat.astype(BF16).reshape(GROUPS, CH, LANES)
    grad_in = swap(s.gf, s.gh, sem.s2a)
    branch_in = swap(s.br, s.bo, sem.s2b)

    landed(core_in)
    x_in = {}

    def rows_of(q):
        return pl.ds(pl.multiple_of(lax.rem(lax.div(at.y, 2) + q, 4) * 2 * BLOCK, 2 * BLOCK), 2 * BLOCK)

    for k in (2, 1, 3, 0):
        part = lax.rem(at.x + k, NX)
        total = s.grads[at.core, part] + s.rcore[part].astype(F32)
        if k == 0:
            s.sx[...] = total
            continue
        s.tx[k] = total.astype(BF16)
        for q in PAIRS:
            x_in[k, q] = go(s.tx.at[k, rows_of(q)], s.rx.at[k, q], sem.x, k * 4 + q, at.along_x(k))

    landed(grad_in)
    outer_spread(s.gh, s.kb, s.border)
    far, border_in = first_along_z(s.border, s.bz, sem.bz)
    inner_spread(s.gh, s.go, s.kb, s.gb, s.acc)
    then_along_z(far, border_in, s.bz, sem.bz)

    y_in = []
    odd = lax.rem(at.y, 2)
    for q in PAIRS:
        landed([x_in[k, q] for k in (1, 3, 2)])
        total = s.sx[rows_of(q)]
        for k in range(1, NX):
            total = total + s.rx[k, q].astype(F32)
        s.ty[q] = total.astype(BF16)
        if q == 0:
            s.sp[...] = total
        for e in (0, 1) if q else (1 - odd,):
            step = lax.rem(lax.rem(lax.div(at.y, 2) + q, 4) * 2 + e - at.y + NY, NY)
            half = pl.ds(pl.multiple_of(e * BLOCK, BLOCK), BLOCK)
            y_in.append(go(s.ty.at[q, half], s.ry.at[step], sem.y, step, at.along_y(step)))

    s.kown[0] = tap_sums(s.pb, s.gb, s.ka)
    taps_far = [go(s.kown.at[0], s.kz.at[j], sem.kz, j, at.along_z(4 * j)) for j in (1, 2)]

    landed(branch_in)
    for g in range(GROUPS):
        span = slice(LANES * g, LANES * (g + 1))
        out_ref[:, span] = (s.x[:, span].astype(F32) + s.bo[g].astype(F32)).astype(BF16)

    landed(y_in)
    total = s.sp[pl.ds(pl.multiple_of(odd * BLOCK, BLOCK), BLOCK)]
    for step in range(1, NY):
        total = total + s.ry[step].astype(F32)
    s.tz[...] = total.astype(BF16)
    s.rz[0] = s.tz[...]
    sum_far = [go(s.tz, s.rz.at[j], sem.sz, j, at.along_z(4 * j)) for j in (1, 2)]
    landed(taps_far)
    s.kown[1] = s.kown[0] + s.kz[1] + s.kz[2]
    taps_near = [go(s.kown.at[1], s.kz.at[2 + m], sem.kz, 2 + m, at.along_z(Z_STEPS[m])) for m in (2, 1, 3)]

    landed(border_in)
    border_xy = []
    for k in (6, 2, 5, 7, 1, 3, 4, 0):
        tile = at.tile_xy(k)
        packed = jnp.zeros((16, LANES), BF16)
        for i in range(4):
            s.bout[k, i] = s.bz[z_slot(at.z, nb_ref[7 - EDGE_DIRS[i], tile]), i]
            corner = s.bz[z_slot(at.z, nb_ref[7 - CORNER_DIRS[i], tile]), 4]
            packed = jnp.where((lane >> 2) & 15 == i, corner, packed)
        s.bout[k, 4] = packed
        if k:
            border_xy.append(go(s.bout.at[k], s.bgot.at[k], sem.bxy, k, at.along_xy(k)))
    s.bgot[0] = s.bout[0]

    landed(sum_far)
    total = jnp.zeros((BLOCK, FULL), F32)
    for third in range(3):
        total = total + s.rz[lax.rem(lax.div(at.z, 4) - third + 3, 3)].astype(F32)
    s.uz[...] = total.astype(BF16)
    s.rz[3] = s.uz[...]
    sum_near = [go(s.uz, s.rz.at[3 + m], sem.sz, 2 + m, at.along_z(Z_STEPS[m])) for m in (2, 1, 3)]

    landed(taps_near)
    s.kown[2] = s.kown[1] + s.kz[3] + s.kz[4] + s.kz[5]
    taps_xy = [go(s.kown.at[2], s.kxy.at[k], sem.kxy, k, at.along_xy(k)) for k in range(1, NXY)]

    landed(sum_near)
    total = jnp.zeros((BLOCK, FULL), F32)
    for quarter in range(4):
        total = total + s.rz[3 + ((at.z - quarter + 4) & 3)].astype(F32)
    all_ref[at.core, at.x, at.y] = (total * SCALE).astype(BF16)
    own = all_ref.at[at.core, at.x, at.y]
    y_all = {k: go(own, own, sem.ay, k, at.along_y(k)) for k in NEAR}
    x_all, core_all = {}, []

    def onward(step):
        block = all_ref.at[at.core, at.x, lax.rem(at.y - step + NY, NY)]
        for k in (2, 1, 3):
            x_all[k, step] = go(block, block, sem.ax, k * NY + step, at.along_x(k))

    onward(0)

    for step in NEAR[:2]:
        landed([y_all[step]])
        onward(step)
    landed(taps_xy)
    total = s.kown[2]
    for k in range(1, NXY):
        total = total + s.kxy[k]
    s.kown[3] = total * SCALE
    kall_ref[at.chan] = s.kown[3]
    taps_all = [go(s.kown.at[3], kall_ref.at[at.chan], sem.kc, k, at.along_chan(k)) for k in range(1, NCHAN)]
    for step in NEAR[2:]:
        landed([y_all[step]])
        onward(step)

    for k in (0, 1, 3, 2):
        if k:
            landed([x_all[k, step] for step in (0, *NEAR)])
        row = all_ref.at[at.core, lax.rem(at.x - k + NX, NX)]
        core_all.append(go(row, row, sem.ac, k, at.partner()))
    landed(border_xy)
    low = lane < 64
    received = []
    packed = jnp.zeros((16, LANES), F32)
    for i in range(4):
        slot = lax.rem(at.xy - lax.div(nb_ref[7 - EDGE_DIRS[i], at.tile], NZ) + NXY, NXY)
        received.append(s.bgot[slot, i].astype(F32))
        slot = lax.rem(at.xy - lax.div(nb_ref[7 - CORNER_DIRS[i], at.tile], NZ) + NXY, NXY)
        packed = jnp.where((lane >> 2) & 15 == i, s.bgot[slot, 4].astype(F32), packed)
    total = dot(unfold(packed), s.places[2])
    for pair in range(2):
        one, two = received[2 * pair : 2 * pair + 2]
        both = [jnp.where(low, one, roll(two, 64)), jnp.where(low, roll(one, 64), two)]
        total = total + dot(jnp.concatenate(both, axis=0).astype(BF16), s.places[pair])
    for g in range(GROUPS):
        span = slice(LANES * g, LANES * (g + 1))
        gin_ref[:, span] = (s.acc[g] + total[:, span]).astype(BF16)
    landed(taps_all)
    landed(core_all)
    for copy in copies:
        copy.wait_send()


def last_kernel(out_ref, gin_ref, all_ref, kall_ref, out2_ref, gin2_ref, win_ref, wout_ref, kgrad_ref):
    out2_ref[...] = out_ref[...]
    gin2_ref[...] = gin_ref[...]
    for x in range(NX):
        for y in range(NY):
            row = FULL * x + BLOCK * y
            wout_ref[row : row + BLOCK, :] = all_ref[0, x, y].astype(F32)
            win_ref[BLOCK * y : BLOCK * (y + 1), FULL * x : FULL * (x + 1)] = all_ref[1, x, y].astype(F32)
    low = iota((8, LANES), 1) >> 5
    for j in range(4):
        for side in range(2):
            rows = jnp.zeros((8, LANES), F32)
            for k in range(4):
                rows = jnp.where(low == k, roll(kall_ref[4 * side + k], 32 * (k - j)), rows)
            for i in range(7):
                if 4 * i + j < TAPS:
                    kgrad_ref[4 * i + j : 4 * i + j + 1, LANES * side : LANES * (side + 1)] = rows[i : i + 1]


def body(inputs, grad_out, kernel, w_in, w_out, neighbours, rotations):
    vmem, semaphores = scratch_shapes()
    tables = [pltpu.SMEM((8, NXY * NZ), I32)] * 2
    scratch = [pltpu.SemaphoreType.DMA((7,)), *tables] + [pltpu.VMEM(shape, dtype) for shape, dtype in vmem.values()]
    for count in semaphores.values():
        scratch += [pltpu.SemaphoreType.DMA((count,))] * 2
    shapes = [((CH, 1024), BF16), ((CH, 1024), BF16), ((2, NX, NY, BLOCK, FULL), BF16), ((NCHAN, 8, LANES), F32)]
    arrays = (neighbours.T, rotations.T, inputs.reshape(CH, 1024), grad_out.reshape(CH, 1024), kernel, w_in, w_out)
    results = pl.pallas_call(
        step_kernel,
        out_shape=[jax.ShapeDtypeStruct(shape, dtype) for shape, dtype in shapes],
        in_specs=[pl.BlockSpec(memory_space=pltpu.HBM)] * 7,
        out_specs=[VMEM] * 4,
        scratch_shapes=scratch,
        compiler_params=pltpu.CompilerParams(vmem_limit_bytes=50 << 20, collective_id=1, has_side_effects=True),
        name="step",
    )(*[pltpu.with_memory_space_constraint(array, pltpu.HBM) for array in arrays])
    shapes = [((CH, 1024), BF16), ((CH, 1024), BF16), ((FULL, HID), F32), ((HID, FULL), F32), ((TAPS, FULL), F32)]
    outputs, grad_in, grad_w_in, grad_w_out, grad_kernel = pl.pallas_call(
        last_kernel,
        out_shape=[jax.ShapeDtypeStruct(shape, dtype) for shape, dtype in shapes],
        in_specs=[VMEM] * 4,
        out_specs=[VMEM] * 5,
        compiler_params=pltpu.CompilerParams(vmem_limit_bytes=12 << 20),
        name="last",
    )(*results)
    return outputs.reshape(1, CH, 1024), grad_in.reshape(1, CH, 1024), grad_w_in, grad_w_out, grad_kernel


def solution(mesh):
    split = P("tile", "chan", None)
    return jax.shard_map(
        body,
        mesh=mesh,
        in_specs=(split, split, P(None, "chan"), P(), P(), P(), P()),
        out_specs=(split, split, P(), P(), P()),
        check_vma=False,
    )
```

```python
import jax
import jax.numpy as jnp
from jax import lax
from jax.experimental import pallas as pl
from jax.experimental.pallas import tpu as pltpu
from jax.sharding import PartitionSpec as P

NX, NZ, NYL, NYH = 4, 12, 2, 4
NXY = NX * NYL
NY = NYL * NYH
NCHAN = NYH * 2
CH = 32
SIDE = 32
LANES = 128
GROUPS = 8
PADS = SIDE + 4
TAPS = 25
HID = 1024
FULL = 256
SCALE = (NXY * NZ * SIDE * SIDE) ** -0.5
MESH = pl.DeviceIdType.MESH
F32, BF16, I32 = jnp.float32, jnp.bfloat16, jnp.int32

BASE = (0, 0, 0, 3, 1, 2, 2, 2)
EDGE_DIRS = (1, 3, 4, 6)
CORNER_DIRS = (0, 2, 5, 7)

VMEM = pl.BlockSpec(memory_space=pltpu.VMEM)
SMEM = pl.BlockSpec(memory_space=pltpu.SMEM)


def iota(shape, axis):
    return lax.broadcasted_iota(I32, shape, axis)


def roll(values, shift):
    return pltpu.roll(values, shift % LANES, 1)


def dot(a, b, contract=((1,), (0,)), precision=None):
    return lax.dot_general(a, b, (contract, ((), ())), preferred_element_type=F32, precision=precision)


def turned(q, i, j):
    q0, q1, q2, q3 = [(q == k).astype(I32) for k in range(4)]
    rows = q0 * i + q1 * j + q2 * (31 - i) + q3 * (31 - j)
    cols = q0 * j + q1 * (31 - i) + q2 * (31 - j) + q3 * i
    return rows, cols


def fold(wide):
    low = iota((16, LANES), 1) < 64
    return jnp.where(low, wide[:16], roll(wide[16:], 64))


def unfold(tile):
    return jnp.concatenate([tile, roll(tile, 64)], axis=0).astype(BF16)


def spread_taps(k_ref, kb):
    taps = k_ref[...].astype(F32)
    eye = iota((CH, CH), 0) == iota((CH, CH), 1)
    ones = jnp.ones((CH, LANES), BF16)
    for tap in range(TAPS):
        row = jnp.broadcast_to(taps[tap : tap + 1, :], (CH, CH))
        kb[tap] = dot(jnp.where(eye, row, 0.0).astype(BF16), ones)


def rims_of(x_ref, rim):
    p = iota((1024, 256), 0)
    n = iota((1, 256), 1)
    e, line, i = n >> 6, (n >> 5) & 1, n & 31
    px = jnp.where(e == 0, (30 + line) * 32 + i, 0)
    px = jnp.where(e == 1, i * 32 + line, px)
    px = jnp.where(e == 2, line * 32 + i, px)
    px = jnp.where(e == 3, i * 32 + 30 + line, px)
    rims = dot(x_ref[...], jnp.where(p == px, 1.0, 0.0).astype(BF16))
    low = iota((16, LANES), 1) < 64
    for pair in range(2):
        half = rims[:, LANES * pair : LANES * (pair + 1)]
        upper, lower = half[:16], half[16:]
        rim[2 * pair] = jnp.where(low, upper, roll(lower, 64)).astype(BF16)
        rim[2 * pair + 1] = jnp.where(low, roll(upper, 64), lower).astype(BF16)


def make_picks(rot_ref, me, wide, narrow):
    def pick(d, i, j, valid):
        q = rot_ref[d, me]
        si, sj = turned(q, i, j)
        e = (q + BASE[d]) & 3
        along = (e & 1) * si + (1 - (e & 1)) * sj
        line = (1 - (e & 1)) * (si - 30 * (e == 0).astype(I32)) + (e & 1) * (sj - 30 * (e == 3).astype(I32))
        lane = jnp.where(valid, line * 32 + along, -1)
        return jnp.where(iota((LANES, lane.shape[1]), 0) == lane, 1.0, 0.0).astype(BF16)

    n = iota((1, 2 * LANES), 1)
    a, lane = n >> 7, n & 127
    for side, (first, dirs) in enumerate(((30, (0, 1, 2)), (0, (5, 6, 7)))):
        i = first + a
        wide[3 * side] = pick(dirs[0], i, 30 + lane, lane < 2)
        wide[3 * side + 1] = pick(dirs[1], i, lane - 2, (lane >= 2) & (lane < 34))
        wide[3 * side + 2] = pick(dirs[2], i, lane - 34, (lane >= 34) & (lane < 36))
    m = iota((1, LANES), 1)
    narrow[0] = pick(3, m >> 1, 30 + (m & 1), m < 64)
    narrow[1] = pick(4, m >> 1, m & 1, m < 64)


def make_places(nb_ref, rot_ref, me, places):
    k = iota((LANES, 1), 0)
    p = iota((1, 1024), 1)
    m = k & 63
    pixels = []
    for d in EDGE_DIRS:
        q = rot_ref[d, nb_ref[7 - d, me]]
        line, along = ((m >> 5), (m & 31)) if d in (1, 6) else ((m & 1), (m >> 1))
        edge = line + (30 if d in (1, 3) else 0)
        si, sj = turned(q, edge, along) if d in (1, 6) else turned(q, along, edge)
        pixels.append(si * 32 + sj)
    for pair in range(2):
        places[pair] = jnp.where(p == jnp.where(k < 64, pixels[2 * pair], pixels[2 * pair + 1]), 1.0, 0.0).astype(BF16)
    q = jnp.zeros((LANES, 1), I32)
    for index, d in enumerate(CORNER_DIRS):
        q = jnp.where(k >> 2 == index, rot_ref[d, nb_ref[7 - d, me]], q)
    i = ((k >> 1) & 1) + jnp.where(k < 8, 30, 0)
    j = (k & 1) + jnp.where((k >> 2) & 1 == 0, 30, 0)
    si, sj = turned(q, i, j)
    places[2] = jnp.where((p == si * 32 + sj) & (k < 16), 1.0, 0.0).astype(BF16)


def inner_conv(x_ref, kb, pb, part):
    lanes = iota((CH, LANES), 1)
    zero = jnp.zeros((CH, LANES), F32)
    for r in (0, 1, 34, 35):
        for b in range(5):
            pb[b, r] = zero
    for g in range(GROUPS):
        chunk = x_ref[:, LANES * g : LANES * (g + 1)].astype(F32)
        for k in range(4):
            row = jnp.where((lanes >= 2) & (lanes < 34), roll(chunk, 2 - 32 * k), 0.0)
            for b in range(5):
                pb[b, 4 * g + k + 2] = roll(row, -b) if b else row

    def group(g, carry):
        out = zero
        for k in range(4):
            acc = zero
            for a in range(5):
                for b in range(5):
                    acc = acc + kb[5 * a + b] * pb[b, 4 * g + k + a]
            out = jnp.where(lanes >> 5 == k, roll(acc, 32 * k), out)
        part[g] = out
        return carry

    lax.fori_loop(0, GROUPS, group, 0)


def outer_conv(tiles, wide, narrow, kb, part, rows_ref, cols_ref, hid):
    lanes = iota((CH, LANES), 1)
    zero = jnp.zeros((CH, LANES), F32)
    above = dot(tiles[0], wide[0]) + dot(tiles[1], wide[1]) + dot(tiles[2], wide[2])
    below = dot(tiles[5], wide[3]) + dot(tiles[6], wide[4]) + dot(tiles[7], wide[5])
    left, right = dot(tiles[3], narrow[0]), dot(tiles[4], narrow[1])
    rows = (above[:, :LANES], above[:, LANES:], below[:, :LANES], below[:, LANES:])
    for i in range(4):
        rows_ref[i] = rows[i]
    cols_ref[0], cols_ref[1] = left, right
    first, second, last, prior = zero, zero, zero, zero
    for b in range(5):
        r0, r1, r2, r3 = [roll(row, -b) if b else row for row in rows]
        first = first + kb[b] * r0 + kb[5 + b] * r1
        second = second + kb[b] * r1
        prior = prior + kb[20 + b] * r2
        last = last + kb[15 + b] * r2 + kb[20 + b] * r3
    even = lanes & 1 == 0
    low, high = zero, zero
    for a in range(5):
        one = roll(left, -2 * (a - 2))
        low = low + kb[5 * a] * one + jnp.where(even, kb[5 * a + 1] * roll(one, -1), 0.0)
        one = roll(right, -2 * (a - 2))
        high = high + kb[5 * a + 4] * one + jnp.where(even, 0.0, kb[5 * a + 3] * roll(one, 1))
    for g in range(GROUPS):
        extra = zero
        for k in range(4):
            u = 4 * g + k
            extra = jnp.where(lanes >> 1 == 16 * k, roll(low, 32 * k - 2 * u), extra)
            extra = jnp.where(lanes >> 1 == 16 * k + 15, roll(high, 32 * k + 30 - 2 * u), extra)
        total = part[g] + extra
        if g == 0:
            total = total + jnp.where(lanes < 32, first, jnp.where(lanes < 64, roll(second, 32), 0.0))
        if g == GROUPS - 1:
            total = total + jnp.where(lanes >= 96, roll(last, 96), jnp.where(lanes >= 64, roll(prior, 64), 0.0))
        hid[g] = total.astype(BF16)


def complete_rows(rows_ref, cols_ref, pb):
    lanes = iota((CH, LANES), 1)
    left, right = cols_ref[0], cols_ref[1]
    for i, r in enumerate((0, 1, 34, 35)):
        for b in range(5):
            pb[b, r] = roll(rows_ref[i], -b) if b else rows_ref[i]
    for r in range(SIDE):
        row = jnp.where(lanes < 2, roll(left, -2 * r), pb[0, r + 2])
        row = jnp.where(lanes >> 1 == 17, roll(right, 34 - 2 * r), row)
        for b in range(5):
            pb[b, r + 2] = roll(row, -b) if b else row


def outer_spread(gh, kb, border):
    lanes = iota((CH, LANES), 1)
    zero = jnp.zeros((CH, LANES), F32)
    own = lanes < 32
    first, last = gh[0].astype(F32), gh[GROUPS - 1].astype(F32)
    r0, r1 = jnp.where(own, first, 0.0), jnp.where(own, roll(first, -32), 0.0)
    r30, r31 = jnp.where(own, roll(last, -64), 0.0), jnp.where(own, roll(last, -96), 0.0)
    gp = [zero] * 4
    for b in range(5):
        s0, s1, s30, s31 = [roll(row, b) if b else row for row in (r0, r1, r30, r31)]
        gp[0] = gp[0] + kb[b] * s0
        gp[1] = gp[1] + kb[b] * s1 + kb[5 + b] * s0
        gp[2] = gp[2] + kb[15 + b] * s31 + kb[20 + b] * s30
        gp[3] = gp[3] + kb[20 + b] * s31
    head, tail = zero, zero
    for g in range(GROUPS):
        chunk = gh[g].astype(F32)
        for k in range(4):
            r = 4 * g + k
            head = jnp.where(lanes >> 1 == r, roll(chunk, 2 * r - 32 * k), head)
            tail = jnp.where(lanes >> 1 == r, roll(chunk, 2 * r - 32 * k - 30), tail)
    even = lanes & 1 == 0
    left, right = zero, zero
    for a in range(5):
        one = roll(head, 2 * (a - 2))
        left = left + kb[5 * a] * one + jnp.where(even, 0.0, kb[5 * a + 1] * roll(one, 1))
        one = roll(tail, 2 * (a - 2))
        right = right + kb[5 * a + 4] * one + jnp.where(even, kb[5 * a + 3] * roll(one, -1), 0.0)
    top, bottom, corners = zero, zero, zero
    for line in range(2):
        upper, lower = gp[line], gp[2 + line]
        top = jnp.where(lanes >> 5 == line, roll(upper, 32 * line - 2), top)
        bottom = jnp.where(lanes >> 5 == line, roll(lower, 32 * line - 2), bottom)
        for i, (row, start) in enumerate(((upper, 0), (upper, 34), (lower, 0), (lower, 34))):
            corners = jnp.where(lanes >> 1 == 2 * i + line, roll(row, 4 * i + 2 * line - start), corners)
    for i, wide in enumerate((top, left, right, bottom, corners)):
        border[i] = fold(wide).astype(BF16)


def inner_spread(gh, go_ref, kb, gb, acc_ref):
    lanes = iota((CH, LANES), 1)
    zero = jnp.zeros((CH, LANES), F32)
    for r in (0, 1, 34, 35):
        for b in range(5):
            gb[b, r] = zero
    for g in range(GROUPS):
        chunk = gh[g].astype(F32)
        for k in range(4):
            row = jnp.where(lanes < 32, roll(chunk, -32 * k) if k else chunk, 0.0)
            for b in range(5):
                gb[b, 4 * g + k + 2] = row if b == 2 else roll(row, b - 2)
        acc_ref[g] = go_ref[:, LANES * g : LANES * (g + 1)].astype(F32)

    def group(g, carry):
        out = zero
        for k in range(4):
            acc = zero
            for a in range(5):
                for b in range(5):
                    acc = acc + kb[5 * a + b] * gb[b, 4 * g + (k + 4 - a)]
            out = jnp.where(lanes >> 5 == k, roll(acc, 32 * k), out)
        acc_ref[g] = acc_ref[g] + out
        return carry

    lax.fori_loop(0, GROUPS, group, 0)


def tap_sums(pb, gb, ka):
    zero = jnp.zeros((CH, LANES), F32)
    for b in range(5):

        def taps(u, sums, b=b):
            grad = gb[2, u + 2]
            return tuple(sums[a] + grad * pb[b, u + a] for a in range(5))

        sums = lax.fori_loop(0, SIDE, taps, (zero,) * 5)
        for a in range(5):
            ka[5 * a + b] = sums[a]
    for tap in range(TAPS, 28):
        ka[tap] = zero
    totals = dot(jnp.ones((8, LANES), F32), ka[...].reshape(28 * CH, LANES), ((1,), (1,)), lax.Precision.HIGHEST)
    sub = iota((8, LANES), 0)
    out = jnp.zeros((8, LANES), F32)
    for i in range(7):
        out = jnp.where(sub == i, totals[:, LANES * i : LANES * (i + 1)], out)
    return out


class Place:
    def __init__(self):
        self.tile, self.chan = lax.axis_index("tile"), lax.axis_index("chan")
        self.z = lax.rem(self.tile, NZ)
        self.xy = lax.div(self.tile, NZ)
        self.x = lax.rem(self.xy, NX)
        self.yl = lax.div(self.xy, NX)
        self.core = lax.rem(self.chan, 2)
        self.yh = lax.div(self.chan, 2)
        self.y = self.yh * NYL + self.yl

    def at(self, tile, chan):
        return {"tile": tile, "chan": chan}

    def along_z(self, k):
        return self.at(self.xy * NZ + lax.rem(self.z + k, NZ), self.chan)

    def tile_xy(self, k):
        return lax.rem(self.xy + k, NXY) * NZ + self.z

    def along_xy(self, k):
        return self.at(self.tile_xy(k), self.chan)

    def along_x(self, k):
        return self.at((self.yl * NX + lax.rem(self.x + k, NX)) * NZ + self.z, self.chan)

    def along_yl(self, k):
        return self.at((lax.rem(self.yl + k, NYL) * NX + self.x) * NZ + self.z, self.chan)

    def along_y(self, k):
        y = lax.rem(self.y + k, NY)
        return self.at((lax.rem(y, NYL) * NX + self.x) * NZ + self.z, lax.div(y, NYL) * 2 + self.core)

    def along_chan(self, k):
        return self.at(self.tile, lax.rem(self.chan + k, NCHAN))

    def partner(self):
        return self.at(self.tile, self.yh * 2 + (1 - self.core))


def send(src, dst, sems, k, device):
    copy = pltpu.make_async_remote_copy(
        src_ref=src, dst_ref=dst, send_sem=sems[0].at[k], recv_sem=sems[1].at[k], device_id=device, device_id_type=MESH
    )
    copy.start()
    return copy


def landed(copies):
    for copy in copies:
        copy.wait_recv()


def z_slot(z, tile):
    behind = lax.rem(z - lax.rem(tile, NZ) + NZ, NZ)
    m = behind & 3
    return m * 3 + lax.rem((behind >> 2) + ((m + 1) >> 2), 3)


Z_STEPS = (0, 1, 2, 11)
BLOCK = 32
NEAR = (1, 7, 2, 6, 3, 5, 4)
PAIRS = (2, 1, 3, 0)


def scratch_shapes():
    rows, tile = (CH, LANES), (16, LANES)
    vmem = dict(
        x=((CH, 1024), BF16), go=((CH, 1024), BF16), taps=((TAPS, CH), BF16), win=((FULL, HID), BF16), wout=((HID, FULL), BF16),
        rim=((4, *tile), BF16), zbuf=((NZ, 4, *tile), BF16), xout=((NXY, 5, *tile), BF16), xgot=((NXY, 5, *tile), BF16),
        wide=((6, LANES, 2 * LANES), BF16), narrow=((2, LANES, LANES), BF16), places=((3, LANES, 1024), BF16),
        kb=((TAPS, *rows), F32), pb=((5, PADS, *rows), F32), gb=((5, PADS, *rows), F32), ka=((28, *rows), F32),
        part=((GROUPS, *rows), F32), rows=((4, *rows), F32), cols=((2, *rows), F32), acc=((GROUPS, *rows), F32),
        hid=((GROUPS, *rows), BF16), feat=((GROUPS, *rows), BF16), cot=((GROUPS, *rows), BF16),
        br=((GROUPS, *rows), BF16), gf=((GROUPS, *rows), BF16), bo=((GROUPS, *rows), BF16), gh=((GROUPS, *rows), BF16),
        border=((5, *tile), BF16), bz=((NZ, 5, *tile), BF16), bout=((NXY, 5, *tile), BF16), bgot=((NXY, 5, *tile), BF16),
        kown=((4, 8, LANES), F32), kz=((6, 8, LANES), F32), kxy=((NXY, 8, LANES), F32),
        grads=((2, NX, FULL, FULL), F32), terms=((2, NX, FULL, FULL), BF16), rcore=((NX, FULL, FULL), BF16),
        sx=((FULL, FULL), F32), tx=((NX, FULL, FULL), BF16), rx=((NX, 4, 2 * BLOCK, FULL), BF16),
        sp=((2 * BLOCK, FULL), F32), ty=((4, 2 * BLOCK, FULL), BF16), ry=((NY, BLOCK, FULL), BF16),
        tz=((BLOCK, FULL), BF16), uz=((BLOCK, FULL), BF16), rz=((7, BLOCK, FULL), BF16),
    )
    sems = dict(
        z=NZ, cot=NCHAN, xy=NXY, s1=NCHAN, s2a=NCHAN, s2b=NCHAN, core=NX, x=NX * 4, y=NY, sz=6, bz=NZ, bxy=NXY,
        kz=6, kxy=NXY, kc=NCHAN, ay=NY, ax=NX * NY, ac=NX,
    )
    return vmem, sems


class Names:
    pass


def step_kernel(
    nb_hbm, rot_hbm, x_hbm, go_hbm, k_hbm, win_hbm, wout_hbm, out_ref, gin_ref, all_ref, kall_ref, load_sem, nb_ref, rot_ref, *rest
):
    vmem, semaphores = scratch_shapes()
    s, sem = Names(), Names()
    for name, ref in zip(vmem, rest):
        setattr(s, name, ref)
    rest = rest[len(vmem) :]
    for index, name in enumerate(semaphores):
        setattr(sem, name, rest[2 * index : 2 * index + 2])
    at = Place()
    copies = []

    def go(*args):
        copies.append(send(*args))
        return copies[-1]

    def first_along_z(src, slots, sems):
        slots[0] = src[...]
        far = [go(src, slots.at[j], sems, j, at.along_z(4 * j)) for j in (1, 2)]
        return far, [go(src, slots.at[3 * m], sems, 3 * m, at.along_z(Z_STEPS[m])) for m in (2, 1, 3)]

    def then_along_z(far, near, slots, sems):
        for j in (1, 2):
            landed([far[j - 1]])
            near += [go(slots.at[j], slots.at[3 * m + j], sems, 3 * m + j, at.along_z(Z_STEPS[m])) for m in (2, 1, 3)]

    barrier = pltpu.get_barrier_semaphore()
    peers = (
        [at.along_z(k) for k in (1, 2, 4, 8, 10, 11)]
        + [at.along_xy(k) for k in range(1, NXY)]
        + [at.along_chan(k) for k in range(1, NCHAN)]
        + [at.along_y(k) for k in range(1, NY)]
    )
    for device in peers:
        pl.semaphore_signal(barrier, inc=1, device_id=device, device_id_type=MESH)
    pairs = ((x_hbm, s.x), (go_hbm, s.go), (k_hbm, s.taps), (win_hbm, s.win), (wout_hbm, s.wout), (nb_hbm, nb_ref), (rot_hbm, rot_ref))
    loads = [pltpu.make_async_copy(src, dst, load_sem.at[i]) for i, (src, dst) in enumerate(pairs)]
    for load in loads:
        load.start()
    loads[0].wait()
    rims_of(s.x, s.rim)
    loads[1].wait()
    pl.semaphore_wait(barrier, len(peers))

    far, z_in = first_along_z(s.rim, s.zbuf, sem.z)
    cot_in = []
    for k in range(1, NCHAN):
        chan = lax.rem(at.chan + k, NCHAN)
        chunk = s.go.at[:, pl.ds(pl.multiple_of(chan * LANES, LANES), LANES)]
        cot_in.append(go(chunk, s.cot.at[at.chan], sem.cot, k, at.along_chan(k)))
    s.cot[at.chan] = s.go[:, pl.ds(pl.multiple_of(at.chan * LANES, LANES), LANES)]
    for load in (loads[2], loads[5], loads[6]):
        load.wait()
    spread_taps(s.taps, s.kb)
    make_picks(rot_ref, at.tile, s.wide, s.narrow)
    then_along_z(far, z_in, s.zbuf, sem.z)
    inner_conv(s.x, s.kb, s.pb, s.part)
    landed(z_in)
    lane = iota((16, LANES), 1)
    xy_in = []
    for k in (6, 2, 5, 7, 1, 3, 4, 0):
        tile = at.tile_xy(k)
        packed = jnp.zeros((16, LANES), F32)
        for i in range(4):
            d = EDGE_DIRS[i]
            s.xout[k, i] = s.zbuf[z_slot(at.z, nb_ref[d, tile]), (rot_ref[d, tile] + BASE[d]) & 3]
            d = CORNER_DIRS[i]
            edge = s.zbuf[z_slot(at.z, nb_ref[d, tile]), (rot_ref[d, tile] + BASE[d]) & 3].astype(F32)
            packed = jnp.where(((lane + 2) & 31) >> 2 == i, roll(edge, 4 * i) if i else edge, packed)
        s.xout[k, 4] = packed.astype(BF16)
        if k:
            xy_in.append(go(s.xout.at[k], s.xgot.at[k], sem.xy, k, at.along_xy(k)))
    s.xgot[0] = s.xout[0]
    make_places(nb_ref, rot_ref, at.tile, s.places)
    loads[3].wait()
    loads[4].wait()
    landed(xy_in)
    tiles = [None] * 8
    for i in range(4):
        d = EDGE_DIRS[i]
        slot = lax.rem(at.xy - lax.div(nb_ref[d, at.tile], NZ) + NXY, NXY)
        tiles[d] = unfold(s.xgot[slot, i].astype(F32))
        d = CORNER_DIRS[i]
        slot = lax.rem(at.xy - lax.div(nb_ref[d, at.tile], NZ) + NXY, NXY)
        packed = s.xgot[slot, 4].astype(F32)
        tiles[d] = unfold(roll(packed, -4 * i) if i else packed)
    outer_conv(tiles, s.wide, s.narrow, s.kb, s.part, s.rows, s.cols, s.hid)

    def swap(src, dst, sems):
        moved = []
        for k in (4, 5, 3, 6, 2, 7, 1):
            chan = lax.rem(at.chan + k, NCHAN)
            moved.append(go(src.at[chan], dst.at[at.chan], sems, k, at.along_chan(k)))
        dst[at.chan] = src[at.chan]
        return moved

    feat_in = swap(s.hid, s.feat, sem.s1)
    complete_rows(s.rows, s.cols, s.pb)
    landed(cot_in)
    landed(feat_in)

    feat = s.feat[...].reshape(FULL, LANES)
    cot = s.cot[...].reshape(FULL, LANES)
    branch = jnp.zeros((FULL, LANES), F32)
    gfeat = jnp.zeros((FULL, LANES), F32)
    core_in = []
    for part in range(NX):
        lo = FULL * part
        w_in = s.win[:, lo : lo + FULL]
        w_out = s.wout[lo : lo + FULL, :]
        pre = dot(w_in, feat, ((0,), (0,)))
        cumul = 0.5 * (1.0 + lax.erf(pre * 0.7071067811865476))
        act = (pre * cumul).astype(BF16)
        gact = dot(w_out, cot)
        slope = cumul + pre * jnp.exp(-0.5 * pre * pre) * 0.3989422804014327
        gpre = (gact * slope).astype(BF16)
        branch = branch + dot(w_out, act, ((0,), (0,)))
        gfeat = gfeat + dot(w_in, gpre)
        for side, value in enumerate((dot(act, cot, ((1,), (1,))), dot(feat, gpre, ((1,), (1,))))):
            s.grads[side, part] = value
            s.terms[side, part] = value.astype(BF16)
        core_in.append(go(s.terms.at[1 - at.core, part], s.rcore.at[part], sem.core, part, at.partner()))
    s.br[...] = branch.astype(BF16).reshape(GROUPS, CH, LANES)
    s.gf[...] = gfeat.astype(BF16).reshape(GROUPS, CH, LANES)
    grad_in = swap(s.gf, s.gh, sem.s2a)
    branch_in = swap(s.br, s.bo, sem.s2b)

    landed(core_in)
    x_in = {}

    def rows_of(q):
        return pl.ds(pl.multiple_of(lax.rem(lax.div(at.y, 2) + q, 4) * 2 * BLOCK, 2 * BLOCK), 2 * BLOCK)

    for k in (2, 1, 3, 0):
        part = lax.rem(at.x + k, NX)
        total = s.grads[at.core, part] + s.rcore[part].astype(F32)
        if k == 0:
            s.sx[...] = total
            continue
        s.tx[k] = total.astype(BF16)
        for q in PAIRS:
            x_in[k, q] = go(s.tx.at[k, rows_of(q)], s.rx.at[k, q], sem.x, k * 4 + q, at.along_x(k))

    landed(grad_in)
    outer_spread(s.gh, s.kb, s.border)
    far, border_in = first_along_z(s.border, s.bz, sem.bz)
    inner_spread(s.gh, s.go, s.kb, s.gb, s.acc)
    then_along_z(far, border_in, s.bz, sem.bz)

    y_in = []
    odd = lax.rem(at.y, 2)
    for q in PAIRS:
        landed([x_in[k, q] for k in (1, 3, 2)])
        total = s.sx[rows_of(q)]
        for k in range(1, NX):
            total = total + s.rx[k, q].astype(F32)
        s.ty[q] = total.astype(BF16)
        if q == 0:
            s.sp[...] = total
        for e in (0, 1) if q else (1 - odd,):
            step = lax.rem(lax.rem(lax.div(at.y, 2) + q, 4) * 2 + e - at.y + NY, NY)
            half = pl.ds(pl.multiple_of(e * BLOCK, BLOCK), BLOCK)
            y_in.append(go(s.ty.at[q, half], s.ry.at[step], sem.y, step, at.along_y(step)))

    s.kown[0] = tap_sums(s.pb, s.gb, s.ka)
    taps_far = [go(s.kown.at[0], s.kz.at[j], sem.kz, j, at.along_z(4 * j)) for j in (1, 2)]

    landed(branch_in)
    for g in range(GROUPS):
        span = slice(LANES * g, LANES * (g + 1))
        out_ref[:, span] = (s.x[:, span].astype(F32) + s.bo[g].astype(F32)).astype(BF16)

    landed(y_in)
    total = s.sp[pl.ds(pl.multiple_of(odd * BLOCK, BLOCK), BLOCK)]
    for step in range(1, NY):
        total = total + s.ry[step].astype(F32)
    s.tz[...] = total.astype(BF16)
    s.rz[0] = s.tz[...]
    sum_far = [go(s.tz, s.rz.at[j], sem.sz, j, at.along_z(4 * j)) for j in (1, 2)]
    landed(taps_far)
    s.kown[1] = s.kown[0] + s.kz[1] + s.kz[2]
    taps_near = [go(s.kown.at[1], s.kz.at[2 + m], sem.kz, 2 + m, at.along_z(Z_STEPS[m])) for m in (2, 1, 3)]

    landed(border_in)
    border_xy = []
    for k in (6, 2, 5, 7, 1, 3, 4, 0):
        tile = at.tile_xy(k)
        packed = jnp.zeros((16, LANES), BF16)
        for i in range(4):
            s.bout[k, i] = s.bz[z_slot(at.z, nb_ref[7 - EDGE_DIRS[i], tile]), i]
            corner = s.bz[z_slot(at.z, nb_ref[7 - CORNER_DIRS[i], tile]), 4]
            packed = jnp.where((lane >> 2) & 15 == i, corner, packed)
        s.bout[k, 4] = packed
        if k:
            border_xy.append(go(s.bout.at[k], s.bgot.at[k], sem.bxy, k, at.along_xy(k)))
    s.bgot[0] = s.bout[0]

    landed(sum_far)
    total = jnp.zeros((BLOCK, FULL), F32)
    for third in range(3):
        total = total + s.rz[lax.rem(lax.div(at.z, 4) - third + 3, 3)].astype(F32)
    s.uz[...] = total.astype(BF16)
    s.rz[3] = s.uz[...]
    sum_near = [go(s.uz, s.rz.at[3 + m], sem.sz, 2 + m, at.along_z(Z_STEPS[m])) for m in (2, 1, 3)]

    landed(taps_near)
    s.kown[2] = s.kown[1] + s.kz[3] + s.kz[4] + s.kz[5]
    taps_xy = [go(s.kown.at[2], s.kxy.at[k], sem.kxy, k, at.along_xy(k)) for k in range(1, NXY)]

    landed(sum_near)
    total = jnp.zeros((BLOCK, FULL), F32)
    for quarter in range(4):
        total = total + s.rz[3 + ((at.z - quarter + 4) & 3)].astype(F32)
    all_ref[at.core, at.x, at.y] = (total * SCALE).astype(BF16)
    own = all_ref.at[at.core, at.x, at.y]
    y_all = {k: go(own, own, sem.ay, k, at.along_y(k)) for k in NEAR}
    x_all, core_all = {}, []

    def onward(step):
        block = all_ref.at[at.core, at.x, lax.rem(at.y - step + NY, NY)]
        for k in (2, 1, 3):
            x_all[k, step] = go(block, block, sem.ax, k * NY + step, at.along_x(k))

    onward(0)

    for step in NEAR[:2]:
        landed([y_all[step]])
        onward(step)
    for step in NEAR[2:]:
        landed([y_all[step]])
        onward(step)

    landed(taps_xy)
    total = s.kown[2]
    for k in range(1, NXY):
        total = total + s.kxy[k]
    s.kown[3] = total * SCALE
    kall_ref[at.chan] = s.kown[3]
    taps_all = [go(s.kown.at[3], kall_ref.at[at.chan], sem.kc, k, at.along_chan(k)) for k in range(1, NCHAN)]
    for k in (0, 1, 3, 2):
        if k:
            landed([x_all[k, step] for step in (0, *NEAR)])
        row = all_ref.at[at.core, lax.rem(at.x - k + NX, NX)]
        core_all.append(go(row, row, sem.ac, k, at.partner()))
    landed(border_xy)
    low = lane < 64
    received = []
    packed = jnp.zeros((16, LANES), F32)
    for i in range(4):
        slot = lax.rem(at.xy - lax.div(nb_ref[7 - EDGE_DIRS[i], at.tile], NZ) + NXY, NXY)
        received.append(s.bgot[slot, i].astype(F32))
        slot = lax.rem(at.xy - lax.div(nb_ref[7 - CORNER_DIRS[i], at.tile], NZ) + NXY, NXY)
        packed = jnp.where((lane >> 2) & 15 == i, s.bgot[slot, 4].astype(F32), packed)
    total = dot(unfold(packed), s.places[2])
    for pair in range(2):
        one, two = received[2 * pair : 2 * pair + 2]
        both = [jnp.where(low, one, roll(two, 64)), jnp.where(low, roll(one, 64), two)]
        total = total + dot(jnp.concatenate(both, axis=0).astype(BF16), s.places[pair])
    for g in range(GROUPS):
        span = slice(LANES * g, LANES * (g + 1))
        gin_ref[:, span] = (s.acc[g] + total[:, span]).astype(BF16)
    landed(taps_all)
    landed(core_all)
    for copy in copies:
        copy.wait_send()


def last_kernel(out_ref, gin_ref, all_ref, kall_ref, out2_ref, gin2_ref, win_ref, wout_ref, kgrad_ref):
    out2_ref[...] = out_ref[...]
    gin2_ref[...] = gin_ref[...]
    for x in range(NX):
        for y in range(NY):
            row = FULL * x + BLOCK * y
            wout_ref[row : row + BLOCK, :] = all_ref[0, x, y].astype(F32)
            win_ref[BLOCK * y : BLOCK * (y + 1), FULL * x : FULL * (x + 1)] = all_ref[1, x, y].astype(F32)
    low = iota((8, LANES), 1) >> 5
    for j in range(4):
        for side in range(2):
            rows = jnp.zeros((8, LANES), F32)
            for k in range(4):
                rows = jnp.where(low == k, roll(kall_ref[4 * side + k], 32 * (k - j)), rows)
            for i in range(7):
                if 4 * i + j < TAPS:
                    kgrad_ref[4 * i + j : 4 * i + j + 1, LANES * side : LANES * (side + 1)] = rows[i : i + 1]


def body(inputs, grad_out, kernel, w_in, w_out, neighbours, rotations):
    vmem, semaphores = scratch_shapes()
    tables = [pltpu.SMEM((8, NXY * NZ), I32)] * 2
    scratch = [pltpu.SemaphoreType.DMA((7,)), *tables] + [pltpu.VMEM(shape, dtype) for shape, dtype in vmem.values()]
    for count in semaphores.values():
        scratch += [pltpu.SemaphoreType.DMA((count,))] * 2
    shapes = [((CH, 1024), BF16), ((CH, 1024), BF16), ((2, NX, NY, BLOCK, FULL), BF16), ((NCHAN, 8, LANES), F32)]
    arrays = (neighbours.T, rotations.T, inputs.reshape(CH, 1024), grad_out.reshape(CH, 1024), kernel, w_in, w_out)
    results = pl.pallas_call(
        step_kernel,
        out_shape=[jax.ShapeDtypeStruct(shape, dtype) for shape, dtype in shapes],
        in_specs=[pl.BlockSpec(memory_space=pltpu.HBM)] * 7,
        out_specs=[VMEM] * 4,
        scratch_shapes=scratch,
        compiler_params=pltpu.CompilerParams(vmem_limit_bytes=50 << 20, collective_id=1, has_side_effects=True),
        name="step",
    )(*[pltpu.with_memory_space_constraint(array, pltpu.HBM) for array in arrays])
    shapes = [((CH, 1024), BF16), ((CH, 1024), BF16), ((FULL, HID), F32), ((HID, FULL), F32), ((TAPS, FULL), F32)]
    outputs, grad_in, grad_w_in, grad_w_out, grad_kernel = pl.pallas_call(
        last_kernel,
        out_shape=[jax.ShapeDtypeStruct(shape, dtype) for shape, dtype in shapes],
        in_specs=[VMEM] * 4,
        out_specs=[VMEM] * 5,
        compiler_params=pltpu.CompilerParams(vmem_limit_bytes=12 << 20),
        name="last",
    )(*results)
    return outputs.reshape(1, CH, 1024), grad_in.reshape(1, CH, 1024), grad_w_in, grad_w_out, grad_kernel


def solution(mesh):
    split = P("tile", "chan", None)
    return jax.shard_map(
        body,
        mesh=mesh,
        in_specs=(split, split, P(None, "chan"), P(), P(), P(), P()),
        out_specs=(split, split, P(), P(), P()),
        check_vma=False,
    )
```
